256 devices in a mesh: dp: 64 (over x, z, core), mp: 4 (over y).
Axes of the slice: x: 4, y: 4, z: 8, core: 2. Of those that a mesh axis runs over, the one named last changes fastest.
Arguments:
- partials: bfloat16 [64, 8, 640, 1024], P('dp', None, None, 'mp'), may hold values from -16 to 16
- owner: int32 [8], replicated, may hold values from 0 to 63, as said below
- rowblock: int32 [8, 64], replicated, may hold values from 0 to 63, each once within a row
- factor: float32 [64, 640, 2, 640], P('dp', 'mp'), as said below
- basis: float32 [64, 640, 2, 640], P('dp', 'mp'), may hold values from -0.25 to 0.25
- moment1: float32 [64, 2, 640, 1024], P('dp', None, None, 'mp'), may hold values from -1.5 to 1.5
- moment2: float32 [64, 2, 640, 1024], P('dp', None, None, 'mp'), may hold values from 0.001 to 0.02
- master: float32 [64, 2, 640, 1024], P('dp', None, None, 'mp'), may hold values from -6 to 6
Outputs:
- train_weights: float32 [8, 64, 10, 1024], P(None, 'dp', None, 'mp')
- new_basis: float32 [64, 640, 2, 640], P('dp', 'mp')
The draws below stay inside these ranges and needn't reach their ends.
Inputs may be any that keep to these rules, and one draw needn't show every extreme that they name: `owner`: each data group owns at most 2 matrices and one owns exactly 2; the first and the last data group each own a matrix. `rowblock`: each row is a permutation of the data groups' row blocks. `factor`: symmetric in its two 640 dimensions.
All inputs are finite; a program needn't handle non-finite values.
Results may differ from the reference program's by a relative error of at most 0.0003.
Values sent between devices are 32-bit elements; how exact they have to be, the bound alone decides.
No kernel may reach another device: no remote copies, remote signals or barrier semaphores. Data moves between devices by JAX's collectives and lax.ppermute only.
A program may use at most 128 MiB of HBM per device.

```python
import math
import jax
import jax.numpy as jnp
from jax import lax

D = 640
C = 1024
NMAT = 8
SLOTS = 2
NS_ITERS = 4
N_DP = 64


def draw_owner(key, part):
    base = jax.random.fold_in(key, 11)
    key_flip = jax.random.fold_in(base, 1)
    key_middle = jax.random.fold_in(base, 2)
    key_order = jax.random.fold_in(base, 3)
    flip = jax.random.randint(key_flip, (), 0, 2).astype(jnp.int32)
    top_group = jnp.int32(N_DP - 1)
    doubled = flip * top_group
    single = (1 - flip) * top_group
    middle = (jax.random.permutation(key_middle, N_DP - 2) + 1).astype(jnp.int32)
    chosen = jnp.concatenate([jnp.stack([doubled, doubled, single]), middle[:NMAT - 3]]).astype(jnp.int32)
    order = jax.random.permutation(key_order, NMAT)
    return jnp.zeros((NMAT,), jnp.int32).at[order].set(chosen)


def draw_factor(key, part):
    shape = (N_DP, D, SLOTS, D)
    raw = jax.random.normal(jax.random.fold_in(key, 5), shape, jnp.float32)
    symmetric = 0.5 * (raw + jnp.transpose(raw, (0, 3, 2, 1)))
    ident = (jnp.arange(D)[:, None, None] == jnp.arange(D)[None, None, :]).astype(jnp.float32)
    return 3.0 * ident[None] + symmetric * D ** (-0.5)


def strengthened(drawn, stream_key, source, target, shards_of, factor):
    owner, partner = [(jnp.arange(drawn.shape[dim]) // (drawn.shape[dim] // shards_of)).reshape([-1 if axis == dim else 1 for axis in range(drawn.ndim)]) for dim in (source, target)]
    chosen = jax.random.permutation(stream_key, shards_of)[partner]
    strong = (owner == chosen) | (owner == (partner + shards_of // 2) % shards_of)
    return jnp.where(strong, factor * drawn, drawn)


def shard_levels(rng, shape, shards, least, top_value):
    def one(dim, parts):
        heights = jax.random.uniform(jax.random.fold_in(jax.random.fold_in(rng, 6), dim), (parts,), jnp.float32, least / len(shards), top_value / len(shards))
        return jnp.repeat(jnp.exp(heights), shape[dim] // parts).reshape((-1,) + (1,) * (len(shape) - dim - 1))

    gain = one(*shards[0])
    for cut in shards[1:]:
        gain = gain * one(*cut)
    return gain


def bell_draw(rng, extent, width, reach, split=(), kind=jnp.bfloat16):
    gain = shard_levels(rng, extent, split, -0.22, 0.18) if split else 1.0
    drawn = jax.random.normal(rng, extent, jnp.float32) * width * gain
    return jnp.minimum(jnp.maximum(drawn, -reach), reach).astype(kind)


def noise_with(rng, dims, spread, reach, cuts, heavy, kind=jnp.bfloat16):
    drawn = spread * jax.random.normal(rng, dims, jnp.float32)
    if cuts:
        drawn = drawn * shard_levels(rng, dims, cuts, -0.22, 0.18)
    return jnp.clip(strengthened(drawn, jax.random.fold_in(rng, 3), *heavy), -reach, reach).astype(kind)


def setup_inputs(seed: int = 0) -> dict:
    key_list = jax.random.split(jax.random.key(seed), 9)
    partials = noise_with(key_list[0], (N_DP, NMAT, D, C), 1.0, 16.0, ((0, 64), (3, 4)), (0, 2, 64, 4.0))
    owner = draw_owner(jax.random.fold_in(key_list[8], 71), 0)
    rowblock = jax.vmap(lambda own: jax.random.permutation(own, N_DP))(jax.random.split(key_list[2], NMAT)).reshape((NMAT, N_DP)).astype(jnp.int32)
    factor = draw_factor(jax.random.fold_in(key_list[8], 71), 0)
    basis = bell_draw(key_list[4], (N_DP, D, SLOTS, D), D ** -0.5, 0.25, ((0, 64), (1, 4)), jnp.float32)
    moment1 = bell_draw(key_list[5], (N_DP, SLOTS, D, C), 0.1, 1.5, ((0, 64), (3, 4)), jnp.float32)
    moment2 = jnp.clip(jnp.exp(math.log(0.02) - 2.9957322 * jax.random.uniform(key_list[6], (N_DP, SLOTS, D, C), jnp.float32) ** shard_levels(key_list[6], (N_DP, SLOTS, D, C), ((0, 64), (3, 4)), -0.2, 0.2)), 0.001, 0.02)
    master = bell_draw(key_list[7], (N_DP, SLOTS, D, C), 1.0, 6.0, ((0, 64), (3, 4)), jnp.float32)
    return dict(partials=partials, owner=owner, rowblock=rowblock, factor=factor, basis=basis, moment1=moment1, moment2=moment2, master=master)


def slots_of(owner):
    order = jnp.arange(owner.shape[0])
    same = owner[:, None] == owner[None, :]
    earlier = order[None, :] < order[:, None]
    return lax.optimization_barrier(jnp.sum((same & earlier).astype(jnp.int32), axis=1))

def reference(partials, owner, rowblock, factor, basis, moment1, moment2, master):
    top_precision = lax.Precision.HIGHEST

    def accumulate(index, total):
        return total + partials[index].astype(jnp.float32)
    summed = lax.fori_loop(0, N_DP, accumulate, jnp.zeros((NMAT, D, C), jnp.float32))
    query_gradient = summed / N_DP
    slot = slots_of(owner)
    new_basis = jnp.zeros((N_DP, D, SLOTS, D), jnp.float32)
    trained = []
    for matrix in range(NMAT):
        group = owner[matrix]
        place = slot[matrix]
        current = basis[group, :, place, :]
        turned_gradient = jnp.dot(current.T, query_gradient[matrix], precision=top_precision)
        leading_moment = 0.9 * moment1[group, place] + 0.1 * turned_gradient
        trailing_moment = 0.95 * moment2[group, place] + 0.05 * turned_gradient * turned_gradient
        direction = jnp.dot(current, leading_moment / (jnp.sqrt(trailing_moment) + 1e-08), precision=top_precision)
        held = master[group, place]
        weights = held - 0.1 * (direction + 0.1 * held)
        blocks = weights.reshape(N_DP, D // N_DP, C)
        trained.append(jnp.take(blocks, rowblock[matrix], axis=0))
        statistic = 0.95 * factor[group, :, place, :] + 0.05 * jnp.dot(query_gradient[matrix], query_gradient[matrix].T, precision=top_precision)
        power = jnp.dot(statistic, current, precision=top_precision)
        iterate = power / jnp.sqrt(jnp.sum(power * power) + 1e-06)
        for step in range(NS_ITERS):
            inner = jnp.dot(iterate, iterate.T, precision=top_precision)
            squared = jnp.dot(inner, inner, precision=top_precision)
            merged_update = -4.775 * inner + 2.0315 * squared
            iterate = 3.4445 * iterate + jnp.dot(merged_update, iterate, precision=top_precision)
        new_basis = new_basis.at[group, :, place, :].set(iterate)
    return (jnp.stack(trained), new_basis)
```

```python
import jax
import jax.numpy as jnp
from jax import lax
from jax.experimental import pallas as pl
from jax.experimental.pallas import tpu as pltpu
from jax.sharding import PartitionSpec as P

NS_ITERS = 4
NT = (((1,), (1,)), ((), ()))
NN = (((1,), (0,)), ((), ()))


def split(x):
    hi = x.astype(jnp.bfloat16)
    lo = (x - hi.astype(jnp.float32)).astype(jnp.bfloat16)
    return hi, lo


def mm(left, right, dims):
    return lax.dot_general(left, right, dims, preferred_element_type=jnp.float32)


def refresh_kernel(g0, g1, g2, g3, f_ref, b_ref, o_ref, gl, gr, left, right, stack, x_ref):
    d = f_ref.shape[0]
    w = g0.shape[1]
    kc = 4 * w
    for b, g_ref in enumerate((g0, g1, g2, g3)):
        hi, lo = split(g_ref[...])
        gl[:, b * w:(b + 1) * w] = hi
        gl[:, kc + b * w:kc + (b + 1) * w] = hi
        gl[:, 2 * kc + b * w:2 * kc + (b + 1) * w] = lo
        gr[:, b * w:(b + 1) * w] = hi
        gr[:, kc + b * w:kc + (b + 1) * w] = lo
        gr[:, 2 * kc + b * w:2 * kc + (b + 1) * w] = hi

    def put_left(v):
        hi, lo = split(v)
        left[:, :d] = hi
        left[:, d:2 * d] = hi
        left[:, 2 * d:] = lo
        return hi, lo

    def put_right(hi, lo):
        right[:, :d] = hi
        right[:, d:2 * d] = lo
        right[:, 2 * d:] = hi

    def put_stack(hi, lo):
        stack[:d] = hi
        stack[d:2 * d] = lo
        stack[2 * d:] = hi

    outer = mm(gl[...], gr[...], NT)
    put_left(0.95 * f_ref[...] + 0.05 * outer)
    put_stack(*split(b_ref[...]))
    power = mm(left[...], stack[...], NN)
    total = jnp.sum(power * power)
    x_ref[...] = power / jnp.sqrt(jnp.full((1, 1), total + 1e-06, jnp.float32))

    def step(_, carry):
        hi, lo = put_left(x_ref[...])
        put_stack(hi, lo)
        put_right(hi, lo)
        inner = mm(left[...], right[...], NT)
        hi, lo = put_left(inner)
        put_right(hi, lo)
        squared = mm(left[...], right[...], NT)
        put_left(-4.775 * inner + 2.0315 * squared)
        x_ref[...] = 3.4445 * x_ref[...] + mm(left[...], stack[...], NN)
        return carry

    lax.fori_loop(0, NS_ITERS, step, 0)
    o_ref[...] = x_ref[...]


def refresh(pieces, f, b):
    d = f.shape[0]
    kc = 4 * pieces[0].shape[1]
    return pl.pallas_call(
        refresh_kernel,
        out_shape=jax.ShapeDtypeStruct((d, d), jnp.float32),
        in_specs=[pl.BlockSpec(memory_space=pltpu.VMEM)] * 6,
        out_specs=pl.BlockSpec(memory_space=pltpu.VMEM),
        scratch_shapes=[
            pltpu.VMEM((d, 3 * kc), jnp.bfloat16),
            pltpu.VMEM((d, 3 * kc), jnp.bfloat16),
            pltpu.VMEM((d, 3 * d), jnp.bfloat16),
            pltpu.VMEM((d, 3 * d), jnp.bfloat16),
            pltpu.VMEM((3 * d, d), jnp.bfloat16),
            pltpu.VMEM((d, d), jnp.float32),
        ],
        compiler_params=pltpu.CompilerParams(vmem_limit_bytes=40 << 20),
        cost_estimate=pl.CostEstimate(
            flops=6 * 14 * d**3, bytes_accessed=16 * d * d, transcendentals=0
        ),
        name="refresh",
    )(*pieces, f, b)


def body(partials, owner, rowblock, factor, basis, moment1, moment2, master):
    precision = lax.Precision.HIGH
    groups = lax.axis_size("dp")
    cols = lax.axis_size("mp")
    d = lax.axis_index("dp")
    y = lax.axis_index("mp")
    core = d % 2
    count = owner.shape[0]
    slots = factor.shape[2]
    rows = factor.shape[1]
    order = jnp.arange(count)
    same = owner[:, None] == owner[None, :]
    slot = jnp.sum((same & (order[None, :] < order[:, None])).astype(jnp.int32), axis=1)
    mine = (owner[None, :] == d) & (slot[None, :] == jnp.arange(slots)[:, None])
    valid = jnp.any(mine, axis=1)
    my_matrix = jnp.sum(jnp.where(mine, order[None, :], 0), axis=1)

    everyone = [(g, j) for g in range(groups) for j in range(cols)]

    def ring(shift, parity):
        return [
            (g * cols + j, g * cols + (j + shift) % cols)
            for g, j in everyone
            if parity is None or (j - g) % 2 == parity
        ]

    def move(x, shift, parity=None):
        return lax.ppermute(x, ("dp", "mp"), ring(shift, parity))

    def target_slot(at):
        return ((at - core) % cols) // 2

    even = (y - core) % 2 == 0
    own_slot = target_slot(y)
    left_slot = target_slot(y - 1)

    def pick(pair, which):
        return jnp.where(which == 0, pair[0], pair[1])

    def to_targets(pair):
        return (
            pick(pair, own_slot),
            move(pick(pair, left_slot), -1, 1),
            move(pick(pair, 1 - own_slot), 2, 0),
            move(pick(pair, 1 - left_slot), 1, 1),
        )

    def in_order(blocks):
        whole = jnp.concatenate(blocks + blocks, axis=0)
        start = ((cols - y) % cols) * rows
        return lax.dynamic_slice_in_dim(whole, start, cols * rows, 0)

    factor_full = in_order(to_targets((factor[0, :, 0], factor[0, :, 1])))
    basis_rows = jnp.concatenate([basis[0, :, 0], basis[0, :, 1]], axis=1)
    basis_full = in_order(
        (
            basis_rows,
            move(basis_rows, -1),
            move(basis_rows, 2),
            move(basis_rows, 1),
        )
    )
    wide = basis_full.shape[1] // 2
    bases = (basis_full[:, :wide], basis_full[:, wide:])

    summed = lax.psum(partials[0].astype(jnp.float32), "dp")
    gradients = tuple(
        lax.dynamic_index_in_dim(summed, my_matrix[s], 0, keepdims=False) / groups
        for s in range(slots)
    )

    pieces = to_targets(gradients)
    refreshed = refresh(pieces, factor_full, pick(bases, own_slot))

    sent = []
    for s in range(slots):
        turned = lax.dot_general(
            bases[s], gradients[s], (((0,), (0,)), ((), ())), precision=precision
        )
        first = 0.9 * moment1[0, s] + 0.1 * turned
        second = 0.95 * moment2[0, s] + 0.05 * turned * turned
        direction = lax.dot_general(
            bases[s], first / (jnp.sqrt(second) + 1e-08), NN, precision=precision
        )
        held = master[0, s]
        weights = held - 0.1 * (direction + 0.1 * held)
        block_rows = weights.shape[0] // groups
        shaped = weights.reshape(groups, block_rows, weights.shape[1])
        chosen = lax.dynamic_index_in_dim(rowblock, my_matrix[s], 0, keepdims=False)
        sent.append(jnp.take(shaped, chosen, axis=0))
    received = lax.all_to_all(
        jnp.stack(sent, axis=0), "dp", split_axis=1, concat_axis=0, tiled=True
    )
    train_weights = jnp.take(received, owner * slots + slot, axis=0)

    keep = jnp.where(own_slot == 0, valid[0], valid[1])
    refreshed = jnp.where(keep, refreshed, 0.0)

    def row_block(at):
        return lax.dynamic_slice_in_dim(refreshed, ((at + cols) % cols) * rows, rows, 0)

    own = row_block(y)
    from_left = move(row_block(y + 1), 1, 0)
    from_far = move(row_block(y + 2), 2, 0)
    from_right = move(row_block(y - 1), -1, 0)
    near = jnp.where(even, own, from_left)
    far = jnp.where(even, from_far, from_right)
    near_first = jnp.where(even, own_slot, left_slot) == 0
    new_basis = jnp.stack(
        [jnp.where(near_first, near, far), jnp.where(near_first, far, near)], axis=1
    )
    return (train_weights, new_basis[None])


def solution(mesh):
    placed = (
        P("dp", None, None, "mp"),
        P(),
        P(),
        P("dp", "mp", None, None),
        P("dp", "mp", None, None),
        P("dp", None, None, "mp"),
        P("dp", None, None, "mp"),
        P("dp", None, None, "mp"),
    )
    return jax.shard_map(
        body,
        mesh=mesh,
        in_specs=placed,
        out_specs=(P(None, "dp", None, "mp"), P("dp", "mp", None, None)),
        check_vma=False,
    )
```

```python
import jax
import jax.numpy as jnp
from jax import lax
from jax.experimental import pallas as pl
from jax.experimental.pallas import tpu as pltpu
from jax.sharding import PartitionSpec as P


NS_ITERS = 4
SLOTS = 2
NX, NZ, NC = 4, 8, 2
NT = (((1,), (1,)), ((), ()))
NN = (((1,), (0,)), ((), ()))


def split(x):
    hi = x.astype(jnp.bfloat16)
    lo = (x - hi.astype(jnp.float32)).astype(jnp.bfloat16)
    return hi, lo


def mm(left, right, dims):
    return lax.dot_general(left, right, dims, preferred_element_type=jnp.float32)


def refresh_kernel(g0, g1, g2, g3, f_ref, b_ref, o_ref, gl, gr, left, right, stack, x_ref):
    d = f_ref.shape[0]
    w = g0.shape[1]
    kc = 4 * w
    for b, g_ref in enumerate((g0, g1, g2, g3)):
        hi, lo = split(g_ref[...])
        gl[:, b * w:(b + 1) * w] = hi
        gl[:, kc + b * w:kc + (b + 1) * w] = hi
        gl[:, 2 * kc + b * w:2 * kc + (b + 1) * w] = lo
        gr[:, b * w:(b + 1) * w] = hi
        gr[:, kc + b * w:kc + (b + 1) * w] = lo
        gr[:, 2 * kc + b * w:2 * kc + (b + 1) * w] = hi

    def put_left(v):
        hi, lo = split(v)
        left[:, :d] = hi
        left[:, d:2 * d] = hi
        left[:, 2 * d:] = lo
        return hi, lo

    def put_right(hi, lo):
        right[:, :d] = hi
        right[:, d:2 * d] = lo
        right[:, 2 * d:] = hi

    def put_stack(hi, lo):
        stack[:d] = hi
        stack[d:2 * d] = lo
        stack[2 * d:] = hi

    outer = mm(gl[...], gr[...], NT)
    put_left(0.95 * f_ref[...] + 0.05 * outer)
    put_stack(*split(b_ref[...]))
    power = mm(left[...], stack[...], NN)
    total = jnp.sum(power * power)
    x_ref[...] = power / jnp.sqrt(jnp.full((1, 1), total + 1e-06, jnp.float32))

    def step(_, carry):
        hi, lo = put_left(x_ref[...])
        put_stack(hi, lo)
        put_right(hi, lo)
        inner = mm(left[...], right[...], NT)
        hi, lo = put_left(inner)
        put_right(hi, lo)
        squared = mm(left[...], right[...], NT)
        put_left(-4.775 * inner + 2.0315 * squared)
        x_ref[...] = 3.4445 * x_ref[...] + mm(left[...], stack[...], NN)
        return carry

    lax.fori_loop(0, NS_ITERS, step, 0)
    o_ref[...] = x_ref[...]


def refresh(pieces, f, b):
    d = f.shape[0]
    kc = 4 * pieces[0].shape[1]
    return pl.pallas_call(
        refresh_kernel,
        out_shape=jax.ShapeDtypeStruct((d, d), jnp.float32),
        in_specs=[pl.BlockSpec(memory_space=pltpu.VMEM)] * 6,
        out_specs=pl.BlockSpec(memory_space=pltpu.VMEM),
        scratch_shapes=[
            pltpu.VMEM((d, 3 * kc), jnp.bfloat16),
            pltpu.VMEM((d, 3 * kc), jnp.bfloat16),
            pltpu.VMEM((d, 3 * d), jnp.bfloat16),
            pltpu.VMEM((d, 3 * d), jnp.bfloat16),
            pltpu.VMEM((3 * d, d), jnp.bfloat16),
            pltpu.VMEM((d, d), jnp.float32),
        ],
        compiler_params=pltpu.CompilerParams(vmem_limit_bytes=40 << 20),
        cost_estimate=pl.CostEstimate(
            flops=6 * 14 * d**3, bytes_accessed=16 * d * d, transcendentals=0
        ),
        name="refresh",
    )(*pieces, f, b)


def line(x, z, core):
    return (x * NZ + z) * NC + core


def owned_gradients(local, owner, slot, d):
    x, core = d // (NZ * NC), d % NC
    count, rows, cols = local.shape
    part = rows // NZ
    paired = local.reshape(NX, NC, rows, cols)
    others = lax.dynamic_index_in_dim(paired, 1 - core, 1, keepdims=False)
    kept = lax.dynamic_index_in_dim(paired, core, 1, keepdims=False)
    swap = [(line(a, b, c), line(a, b, 1 - c)) for a in range(NX) for b in range(NZ) for c in range(NC)]
    came = lax.ppermute(others.astype(jnp.float32), "dp", swap)
    chip = kept.astype(jnp.float32) + came
    along_x = [[line(a, b, c) for a in range(NX)] for b in range(NZ) for c in range(NC)]
    along_z = [[line(a, b, c) for b in range(NZ)] for a in range(NX) for c in range(NC)]
    across = [[line(a, b, c) for a in range(NX) for c in range(NC)] for b in range(NZ)]

    def exchange(v, lines):
        return lax.all_to_all(v, "dp", 0, 0, axis_index_groups=lines, tiled=True)

    over_x = jnp.sum(exchange(chip, along_x), axis=0)
    over_z = jnp.sum(exchange(over_x.reshape(NZ, part, cols), along_z), axis=0)
    mean = over_z * (1.0 / (NX * NZ * NC))
    everything = exchange(jnp.broadcast_to(mean[None], (count, part, cols)), across)
    groups = NX * NZ * NC
    hits = (owner[None, None, :] == jnp.arange(groups)[:, None, None]) & (
        slot[None, None, :] == jnp.arange(SLOTS)[None, :, None]
    )
    matrix_of = jnp.sum(jnp.where(hits, jnp.arange(count)[None, None, :], 0), axis=2)
    wanted = lax.dynamic_index_in_dim(matrix_of.reshape(NX, NZ, NC, SLOTS), x, 0, keepdims=False)
    wanted = lax.dynamic_index_in_dim(wanted, core, 1, keepdims=False)
    outgoing = jnp.take(everything, wanted.reshape(-1), axis=0, mode="clip")
    incoming = exchange(outgoing.reshape(NZ, SLOTS, part, cols), along_z)
    return tuple(incoming[:, s].reshape(rows, cols) for s in range(SLOTS))


def body(partials, owner, rowblock, factor, basis, moment1, moment2, master):
    precision = lax.Precision.HIGH
    groups = lax.axis_size("dp")
    cols = lax.axis_size("mp")
    d = lax.axis_index("dp")
    y = lax.axis_index("mp")
    core = d % 2
    count = owner.shape[0]
    slots = factor.shape[2]
    rows = factor.shape[1]
    order = jnp.arange(count)
    same = owner[:, None] == owner[None, :]
    slot = jnp.sum((same & (order[None, :] < order[:, None])).astype(jnp.int32), axis=1)
    mine = (owner[None, :] == d) & (slot[None, :] == jnp.arange(slots)[:, None])
    valid = jnp.any(mine, axis=1)
    my_matrix = jnp.sum(jnp.where(mine, order[None, :], 0), axis=1)

    everyone = [(g, j) for g in range(groups) for j in range(cols)]

    def ring(shift, parity):
        return [
            (g * cols + j, g * cols + (j + shift) % cols)
            for g, j in everyone
            if parity is None or (j - g) % 2 == parity
        ]

    def move(x, shift, parity=None):
        return lax.ppermute(x, ("dp", "mp"), ring(shift, parity))

    def target_slot(at):
        return ((at - core) % cols) // 2

    even = (y - core) % 2 == 0
    own_slot = target_slot(y)
    left_slot = target_slot(y - 1)

    def pick(pair, which):
        return jnp.where(which == 0, pair[0], pair[1])

    def to_targets(pair):
        return (
            pick(pair, own_slot),
            move(pick(pair, left_slot), -1, 1),
            move(pick(pair, 1 - own_slot), 2, 0),
            move(pick(pair, 1 - left_slot), 1, 1),
        )

    def in_order(blocks):
        whole = jnp.concatenate(blocks + blocks, axis=0)
        start = ((cols - y) % cols) * rows
        return lax.dynamic_slice_in_dim(whole, start, cols * rows, 0)

    factor_full = in_order(to_targets((factor[0, :, 0], factor[0, :, 1])))
    basis_rows = jnp.concatenate([basis[0, :, 0], basis[0, :, 1]], axis=1)
    basis_full = in_order(
        (
            basis_rows,
            move(basis_rows, -1),
            move(basis_rows, 2),
            move(basis_rows, 1),
        )
    )
    wide = basis_full.shape[1] // 2
    bases = (basis_full[:, :wide], basis_full[:, wide:])

    gradients = owned_gradients(partials[0], owner, slot, d)
    pieces = to_targets(gradients)
    refreshed = refresh(pieces, factor_full, pick(bases, own_slot))

    sent = []
    for s in range(slots):
        turned = lax.dot_general(
            bases[s], gradients[s], (((0,), (0,)), ((), ())), precision=precision
        )
        first = 0.9 * moment1[0, s] + 0.1 * turned
        second = 0.95 * moment2[0, s] + 0.05 * turned * turned
        direction = lax.dot_general(
            bases[s], first / (jnp.sqrt(second) + 1e-08), NN, precision=precision
        )
        held = master[0, s]
        weights = held - 0.1 * (direction + 0.1 * held)
        block_rows = weights.shape[0] // groups
        shaped = weights.reshape(groups, block_rows, weights.shape[1])
        chosen = lax.dynamic_index_in_dim(rowblock, my_matrix[s], 0, keepdims=False)
        sent.append(jnp.take(shaped, chosen, axis=0))
    received = lax.all_to_all(
        jnp.stack(sent, axis=0), "dp", split_axis=1, concat_axis=0, tiled=True
    )
    train_weights = jnp.take(received, owner * slots + slot, axis=0)

    keep = jnp.where(own_slot == 0, valid[0], valid[1])
    refreshed = jnp.where(keep, refreshed, 0.0)

    def row_block(at):
        return lax.dynamic_slice_in_dim(refreshed, ((at + cols) % cols) * rows, rows, 0)

    own = row_block(y)
    from_left = move(row_block(y + 1), 1, 0)
    from_far = move(row_block(y + 2), 2, 0)
    from_right = move(row_block(y - 1), -1, 0)
    near = jnp.where(even, own, from_left)
    far = jnp.where(even, from_far, from_right)
    near_first = jnp.where(even, own_slot, left_slot) == 0
    new_basis = jnp.stack(
        [jnp.where(near_first, near, far), jnp.where(near_first, far, near)], axis=1
    )
    return (train_weights, new_basis[None])


def solution(mesh):
    placed = (
        P("dp", None, None, "mp"),
        P(),
        P(),
        P("dp", "mp", None, None),
        P("dp", "mp", None, None),
        P("dp", None, None, "mp"),
        P("dp", None, None, "mp"),
        P("dp", None, None, "mp"),
    )
    return jax.shard_map(
        body,
        mesh=mesh,
        in_specs=placed,
        out_specs=(P(None, "dp", None, "mp"), P("dp", "mp", None, None)),
        check_vma=False,
    )
```

```python
import jax
import jax.numpy as jnp
from jax import lax
from jax.experimental import pallas as pl
from jax.experimental.pallas import tpu as pltpu
from jax.sharding import PartitionSpec as P


NS_ITERS = 4
SLOTS = 2
PARTS = (80,)
NX, NZ, NC = 4, 8, 2
NT = (((1,), (1,)), ((), ()))
NN = (((1,), (0,)), ((), ()))


def split(x):
    hi = x.astype(jnp.bfloat16)
    lo = (x - hi.astype(jnp.float32)).astype(jnp.bfloat16)
    return hi, lo


def mm(left, right, dims):
    return lax.dot_general(left, right, dims, preferred_element_type=jnp.float32)


def mm3(left, right, dims=NN):
    (lh, ll), (rh, rl) = left, right
    return mm(lh, rh, dims) + (mm(lh, rl, dims) + mm(ll, rh, dims))


def row_starts(y, rows, cols):
    return [pl.multiple_of(lax.rem(y + k, cols) * rows, 32) for k in range(cols)]


def scattered(part):
    lead = sum(PARTS[:part])
    whole = sum(PARTS)
    return [(z * PARTS[part], z * whole + lead, PARTS[part]) for z in range(NZ)]


def prepare_kernel(at, b0, b1, b2, b3, hi_ref, lo_ref, thi_ref, tlo_ref, whole):
    blocks = (b0, b1, b2, b3)
    rows, d = b0.shape[0], whole.shape[0]
    starts = row_starts(at[0], rows, len(blocks))
    for s in range(SLOTS):
        for start, block in zip(starts, blocks):
            whole[pl.ds(start, rows), :] = block[:, s * d:(s + 1) * d]
        b = whole[...]
        hi_ref[s], lo_ref[s] = split(b)
        thi_ref[s], tlo_ref[s] = split(b.T)


def prepare(scalars, blocks):
    d = blocks[0].shape[1] // SLOTS
    half = jax.ShapeDtypeStruct((SLOTS, d, d), jnp.bfloat16)
    vmem = pl.BlockSpec(memory_space=pltpu.VMEM)
    return pl.pallas_call(
        prepare_kernel,
        out_shape=[half] * 4,
        in_specs=[pl.BlockSpec(memory_space=pltpu.SMEM)] + [vmem] * 4,
        out_specs=[vmem] * 4,
        scratch_shapes=[pltpu.VMEM((d, d), jnp.float32)],
        compiler_params=pltpu.CompilerParams(vmem_limit_bytes=24 << 20),
        cost_estimate=pl.CostEstimate(flops=8 * d * d, bytes_accessed=24 * d * d, transcendentals=0),
        name="prepare",
    )(scalars, *blocks)


def update_kernel(chosen, *refs):
    incoming = refs[:len(PARTS)]
    hi, lo, thi, tlo, m1, m2, held, out, gh, gl, weights = refs[len(PARTS):]
    groups = out.shape[0]
    block = held.shape[1] // groups
    for s in range(SLOTS):
        for part, ref in enumerate(incoming):
            for z, (_, row, size) in enumerate(scattered(part)):
                gh[row:row + size], gl[row:row + size] = split(ref[z, s])
        turned = mm3((thi[s], tlo[s]), (gh[...], gl[...]))
        first = 0.9 * m1[s] + 0.1 * turned
        second = 0.95 * m2[s] + 0.05 * turned * turned
        direction = mm3((hi[s], lo[s]), split(first / (jnp.sqrt(second) + 1e-08)))
        fresh = held[s] - 0.1 * (direction + 0.1 * held[s])
        here = slice(s * block, (s + 1) * block)
        for j in range(groups):
            weights[j, here, :] = fresh[j * block:(j + 1) * block]

        def send(j, carry):
            out[j, here, :] = weights[chosen[s, j], here, :]
            return carry

        lax.fori_loop(0, groups, send, 0, unroll=4)


def update(chosen, incoming, halves, m1, m2, held):
    groups = chosen.shape[1]
    d, cols = m1.shape[1:]
    block = d // groups
    padded = -(-SLOTS * block // 8) * 8
    vmem = pl.BlockSpec(memory_space=pltpu.VMEM)
    return pl.pallas_call(
        update_kernel,
        out_shape=jax.ShapeDtypeStruct((groups, padded, cols), jnp.float32),
        in_specs=[pl.BlockSpec(memory_space=pltpu.SMEM)] + [vmem] * (7 + len(PARTS)),
        out_specs=vmem,
        scratch_shapes=[
            pltpu.VMEM((d, cols), jnp.bfloat16),
            pltpu.VMEM((d, cols), jnp.bfloat16),
            pltpu.VMEM((groups, padded, cols), jnp.float32),
        ],
        compiler_params=pltpu.CompilerParams(vmem_limit_bytes=24 << 20),
        cost_estimate=pl.CostEstimate(
            flops=24 * d * d * cols, bytes_accessed=36 * d * cols, transcendentals=2 * d * cols
        ),
        name="update",
    )(chosen, *incoming, *halves, m1, m2, held)


def refresh_kernel(at, g0, g1, g2, g3, f0, f1, f2, f3, b_hi, b_lo, o_ref, gl, gr, left, right, stack, x_ref):
    d = x_ref.shape[0]
    w = g0.shape[1]
    kc = 4 * w
    for b, g_ref in enumerate((g0, g1, g2, g3)):
        base = 0
        for part in range(len(PARTS)):
            for source, row, size in scattered(part):
                hi, lo = split(g_ref[base + source:base + source + size])
                gl[row:row + size, b * w:(b + 1) * w] = hi
                gl[row:row + size, kc + b * w:kc + (b + 1) * w] = hi
                gl[row:row + size, 2 * kc + b * w:2 * kc + (b + 1) * w] = lo
                gr[row:row + size, b * w:(b + 1) * w] = hi
                gr[row:row + size, kc + b * w:kc + (b + 1) * w] = lo
                gr[row:row + size, 2 * kc + b * w:2 * kc + (b + 1) * w] = hi
            base += NZ * PARTS[part]

    def put_left(v):
        hi, lo = split(v)
        left[:, :d] = hi
        left[:, d:2 * d] = hi
        left[:, 2 * d:] = lo
        return hi, lo

    def put_right(hi, lo):
        right[:, :d] = hi
        right[:, d:2 * d] = lo
        right[:, 2 * d:] = hi

    def put_stack(hi, lo):
        stack[:d] = hi
        stack[d:2 * d] = lo
        stack[2 * d:] = hi

    x_ref[...] = mm(gl[...], gr[...], NT)
    rows = f0.shape[0]
    for start, f_ref in zip(row_starts(at[0], rows, 4), (f0, f1, f2, f3)):
        here = pl.ds(start, rows)
        hi, lo = split(0.95 * f_ref[...] + 0.05 * x_ref[here, :])
        left[here, :d] = hi
        left[here, d:2 * d] = hi
        left[here, 2 * d:] = lo
    put_stack(b_hi[at[1]], b_lo[at[1]])
    power = mm(left[...], stack[...], NN)
    total = jnp.sum(power * power)
    x_ref[...] = power / jnp.sqrt(jnp.full((1, 1), total + 1e-06, jnp.float32))

    def step(_, carry):
        hi, lo = put_left(x_ref[...])
        put_stack(hi, lo)
        put_right(hi, lo)
        inner = mm(left[...], right[...], NT)
        hi, lo = put_left(inner)
        put_right(hi, lo)
        squared = mm(left[...], right[...], NT)
        put_left(-4.775 * inner + 2.0315 * squared)
        x_ref[...] = 3.4445 * x_ref[...] + mm(left[...], stack[...], NN)
        return carry

    lax.fori_loop(0, NS_ITERS, step, 0)
    o_ref[...] = jnp.where(at[2] > 0, x_ref[...], 0.0)


def refresh(scalars, pieces, factors, b_hi, b_lo):
    d = factors[0].shape[1]
    kc = 4 * pieces[0].shape[1]
    vmem = pl.BlockSpec(memory_space=pltpu.VMEM)
    return pl.pallas_call(
        refresh_kernel,
        out_shape=jax.ShapeDtypeStruct((d, d), jnp.float32),
        in_specs=[pl.BlockSpec(memory_space=pltpu.SMEM)] + [vmem] * 10,
        out_specs=vmem,
        scratch_shapes=[
            pltpu.VMEM((d, 3 * kc), jnp.bfloat16),
            pltpu.VMEM((d, 3 * kc), jnp.bfloat16),
            pltpu.VMEM((d, 3 * d), jnp.bfloat16),
            pltpu.VMEM((d, 3 * d), jnp.bfloat16),
            pltpu.VMEM((3 * d, d), jnp.bfloat16),
            pltpu.VMEM((d, d), jnp.float32),
        ],
        compiler_params=pltpu.CompilerParams(vmem_limit_bytes=40 << 20),
        cost_estimate=pl.CostEstimate(
            flops=6 * 14 * d**3, bytes_accessed=16 * d * d, transcendentals=0
        ),
        name="refresh",
    )(scalars, *pieces, *factors, b_hi, b_lo)


def line(x, z, core):
    return (x * NZ + z) * NC + core


def owned_gradients(local, owner, slot, d):
    x, core = d // (NZ * NC), d % NC
    count, rows, cols = local.shape
    groups = NX * NZ * NC
    along_x = [[line(a, b, c) for a in range(NX)] for b in range(NZ) for c in range(NC)]
    along_z = [[line(a, b, c) for b in range(NZ)] for a in range(NX) for c in range(NC)]
    across = [[line(a, b, c) for a in range(NX) for c in range(NC)] for b in range(NZ)]
    swap = [
        (line(a, b, c), line(a, b, 1 - c))
        for a in range(NX) for b in range(NZ) for c in range(NC)
    ]

    def exchange(v, lines):
        return lax.all_to_all(v, "dp", 0, 0, axis_index_groups=lines, tiled=True)

    hits = (owner[None, None, :] == jnp.arange(groups)[:, None, None]) & (
        slot[None, None, :] == jnp.arange(SLOTS)[None, :, None]
    )
    matrix_of = jnp.sum(jnp.where(hits, jnp.arange(count)[None, None, :], 0), axis=2)
    wanted = lax.dynamic_index_in_dim(matrix_of.reshape(NX, NZ, NC, SLOTS), x, 0, keepdims=False)
    wanted = lax.dynamic_index_in_dim(wanted, core, 1, keepdims=False).reshape(-1)

    paired = local.reshape(NX, NC, NZ, rows // NZ, cols)
    others = lax.dynamic_index_in_dim(paired, 1 - core, 1, keepdims=False)
    kept = lax.dynamic_index_in_dim(paired, core, 1, keepdims=False)
    outs = []
    lead = 0
    for size in PARTS:
        came = lax.ppermute(
            others[:, :, lead:lead + size].astype(jnp.float32).reshape(NX, NZ * size, cols), "dp", swap
        )
        chip = kept[:, :, lead:lead + size].astype(jnp.float32).reshape(NX, NZ * size, cols) + came
        lead += size
        outs.append(exchange(chip, along_x))
    incoming = []
    for part, size in enumerate(PARTS):
        over_x = jnp.sum(outs[part], axis=0)
        over_z = jnp.sum(exchange(over_x.reshape(NZ, size, cols), along_z), axis=0)
        mean = over_z * (1.0 / groups)
        everything = exchange(jnp.broadcast_to(mean[None], (count, size, cols)), across)
        outgoing = jnp.take(everything, wanted, axis=0, mode="clip")
        incoming.append(exchange(outgoing.reshape(NZ, SLOTS, size, cols), along_z))
    return incoming


def body(partials, owner, rowblock, factor, basis, moment1, moment2, master):
    groups = lax.axis_size("dp")
    cols = lax.axis_size("mp")
    d = lax.axis_index("dp")
    y = lax.axis_index("mp")
    core = d % NC
    count = owner.shape[0]
    rows = factor.shape[1]
    order = jnp.arange(count)
    same = owner[:, None] == owner[None, :]
    slot = jnp.sum((same & (order[None, :] < order[:, None])).astype(jnp.int32), axis=1)
    mine = (owner[None, :] == d) & (slot[None, :] == jnp.arange(SLOTS)[:, None])
    valid = jnp.any(mine, axis=1)
    my_matrix = jnp.sum(jnp.where(mine, order[None, :], 0), axis=1)

    everyone = [(g, j) for g in range(groups) for j in range(cols)]

    def ring(shift, parity):
        return [
            (g * cols + j, g * cols + (j + shift) % cols)
            for g, j in everyone
            if parity is None or (j - g) % 2 == parity
        ]

    def move(v, shift, parity=None):
        return lax.ppermute(v, ("dp", "mp"), ring(shift, parity))

    def target_slot(at):
        return ((at - core) % cols) // 2

    even = (y - core) % 2 == 0
    own_slot = target_slot(y)
    left_slot = target_slot(y - 1)

    def to_targets(pick):
        return (
            pick(own_slot),
            move(pick(left_slot), -1, 1),
            move(pick(1 - own_slot), 2, 0),
            move(pick(1 - left_slot), 1, 1),
        )

    keep = jnp.where(own_slot == 0, valid[0], valid[1])
    scalars = jnp.stack([y, own_slot, keep.astype(jnp.int32)]).astype(jnp.int32)
    basis_rows = jnp.concatenate([basis[0, :, 0], basis[0, :, 1]], axis=1)
    blocks = (basis_rows, move(basis_rows, -1), move(basis_rows, 2), move(basis_rows, 1))
    halves = prepare(scalars, blocks)
    factors = to_targets(lambda s: jnp.where(s == 0, factor[0, :, 0], factor[0, :, 1]))

    incoming = owned_gradients(partials[0], owner, slot, d)

    def block_of(s):
        return jnp.concatenate(
            [
                jnp.where(s == 0, v[:, 0], v[:, 1]).reshape(-1, v.shape[-1])
                for v in incoming
            ],
            axis=0,
        )

    pieces = to_targets(block_of)
    chosen = jnp.sum(jnp.where(mine[:, :, None], rowblock[None], 0), axis=1)
    sent = update(chosen, incoming, halves, moment1[0], moment2[0], master[0])
    received = lax.all_to_all(sent, "dp", split_axis=0, concat_axis=0, tiled=True)
    refreshed = refresh(scalars, pieces, factors, halves[0], halves[1])

    landed = jnp.take(received, owner, axis=0, mode="clip")
    block_rows = rows * cols // groups
    train_weights = jnp.where(
        (slot == 0)[:, None, None], landed[:, :block_rows], landed[:, block_rows:2 * block_rows]
    )[:, None]

    def row_block(at):
        return lax.dynamic_slice_in_dim(refreshed, ((at + cols) % cols) * rows, rows, 0)

    own = row_block(y)
    from_left = move(row_block(y + 1), 1, 0)
    from_far = move(row_block(y + 2), 2, 0)
    from_right = move(row_block(y - 1), -1, 0)
    near = jnp.where(even, own, from_left)
    far = jnp.where(even, from_far, from_right)
    near_first = jnp.where(even, own_slot, left_slot) == 0
    new_basis = jnp.stack(
        [jnp.where(near_first, near, far), jnp.where(near_first, far, near)], axis=1
    )
    return (train_weights, new_basis[None])


def solution(mesh):
    placed = (
        P("dp", None, None, "mp"),
        P(),
        P(),
        P("dp", "mp", None, None),
        P("dp", "mp", None, None),
        P("dp", None, None, "mp"),
        P("dp", None, None, "mp"),
        P("dp", None, None, "mp"),
    )

    return jax.shard_map(
        body,
        mesh=mesh,
        in_specs=placed,
        out_specs=(P(None, "dp", None, "mp"), P("dp", "mp", None, None)),
        check_vma=False,
    )
```

```python
import jax
import jax.numpy as jnp
from jax import lax
from jax.experimental import pallas as pl
from jax.experimental.pallas import tpu as pltpu
from jax.sharding import PartitionSpec as P


NS_ITERS = 4
SLOTS = 2
BLOCK = 256
VMEM = 63 << 20
PARTS = (80,)
NX, NZ, NC = 4, 8, 2
NT = (((1,), (1,)), ((), ()))
NN = (((1,), (0,)), ((), ()))


def split(x):
    hi = x.astype(jnp.bfloat16)
    lo = (x - hi.astype(jnp.float32)).astype(jnp.bfloat16)
    return hi, lo


def mm(left, right, dims):
    return lax.dot_general(left, right, dims, preferred_element_type=jnp.float32)


def mm3(left, right, dims=NN):
    (lh, ll), (rh, rl) = left, right
    return mm(lh, rh, dims) + (mm(lh, rl, dims) + mm(ll, rh, dims))


def row_starts(y, rows, cols):
    return [pl.multiple_of(lax.rem(y + k, cols) * rows, 32) for k in range(cols)]


def scattered(part):
    lead = sum(PARTS[:part])
    whole = sum(PARTS)
    return [(z * PARTS[part], z * whole + lead, PARTS[part]) for z in range(NZ)]


def start_all(copies):
    for copy in copies:
        copy.start()


def wait_all(copies):
    for copy in copies:
        copy.wait()


def prepare_kernel(at, b0, b1, b2, b3, hi_ref, lo_ref, thi_ref, tlo_ref, held, whole, parts, in_sem, out_sem):
    blocks = (b0, b1, b2, b3)
    rows, d = b0.shape[0], whole.shape[0]
    fetch = [pltpu.make_async_copy(b, held.at[k], in_sem.at[k]) for k, b in enumerate(blocks)]
    start_all(fetch)
    wait_all(fetch)
    starts = row_starts(at[0], rows, len(blocks))
    stores = []
    for s in range(SLOTS):
        for k, start in enumerate(starts):
            whole[pl.ds(start, rows), :] = held[k, :, s * d:(s + 1) * d]
        b = whole[...]
        parts[0, s], parts[1, s] = split(b)
        parts[2, s], parts[3, s] = split(b.T)
        mine = [
            pltpu.make_async_copy(parts.at[k, s], ref.at[s], out_sem.at[k, s])
            for k, ref in enumerate((hi_ref, lo_ref, thi_ref, tlo_ref))
        ]
        start_all(mine)
        stores += mine
    wait_all(stores)


def prepare(scalars, blocks):
    rows, wide = blocks[0].shape
    d = wide // SLOTS
    half = jax.ShapeDtypeStruct((SLOTS, d, d), jnp.bfloat16)
    hbm = pl.BlockSpec(memory_space=pltpu.HBM)
    return pl.pallas_call(
        prepare_kernel,
        out_shape=[half] * 4,
        in_specs=[pl.BlockSpec(memory_space=pltpu.SMEM)] + [hbm] * 4,
        out_specs=[hbm] * 4,
        scratch_shapes=[
            pltpu.VMEM((4, rows, wide), jnp.float32),
            pltpu.VMEM((d, d), jnp.float32),
            pltpu.VMEM((4, SLOTS, d, d), jnp.bfloat16),
            pltpu.SemaphoreType.DMA((4,)),
            pltpu.SemaphoreType.DMA((4, SLOTS)),
        ],
        compiler_params=pltpu.CompilerParams(vmem_limit_bytes=VMEM),
        cost_estimate=pl.CostEstimate(flops=8 * d * d, bytes_accessed=24 * d * d, transcendentals=0),
        name="prepare",
    )(scalars, *blocks)


def update_kernel(chosen, *refs):
    count = len(PARTS)
    incoming, sources, states, out = refs[:count], refs[count:count + 4], refs[count + 4:count + 7], refs[count + 7]
    scratch = refs[count + 8:]
    came, (parts, state, gh, gl, weights, came_sem, part_sem, state_sem) = scratch[:count], scratch[count:]
    groups = out.shape[0]
    block = state.shape[2] // groups
    order = (2, 3, 0, 1)
    get_came = [pltpu.make_async_copy(r, c, came_sem.at[k]) for k, (r, c) in enumerate(zip(incoming, came))]
    get_part = [
        [pltpu.make_async_copy(sources[k].at[s], parts.at[k, s], part_sem.at[k, s]) for k in order]
        for s in range(SLOTS)
    ]
    get_state = [
        [pltpu.make_async_copy(r.at[s], state.at[k, s], state_sem.at[k, s]) for k, r in enumerate(states)]
        for s in range(SLOTS)
    ]
    start_all(get_came)
    for s in range(SLOTS):
        start_all(get_part[s])
        start_all(get_state[s])
    wait_all(get_came)
    for s in range(SLOTS):
        for part, ref in enumerate(came):
            for z, (_, row, size) in enumerate(scattered(part)):
                gh[row:row + size], gl[row:row + size] = split(ref[z, s])
        wait_all(get_part[s][:2])
        turned = mm3((parts[2, s], parts[3, s]), (gh[...], gl[...]))
        wait_all(get_state[s])
        first = 0.9 * state[0, s] + 0.1 * turned
        second = 0.95 * state[1, s] + 0.05 * turned * turned
        wait_all(get_part[s][2:])
        direction = mm3((parts[0, s], parts[1, s]), split(first / (jnp.sqrt(second) + 1e-08)))
        fresh = state[2, s] - 0.1 * (direction + 0.1 * state[2, s])
        here = slice(s * block, (s + 1) * block)
        for j in range(groups):
            weights[j, here, :] = fresh[j * block:(j + 1) * block]

        def send(j, carry):
            out[j, here, :] = weights[chosen[s, j], here, :]
            return carry

        lax.fori_loop(0, groups, send, 0, unroll=4)


def update(chosen, incoming, halves, m1, m2, held):
    groups = chosen.shape[1]
    d, cols = m1.shape[1:]
    block = d // groups
    padded = -(-SLOTS * block // 8) * 8
    hbm = pl.BlockSpec(memory_space=pltpu.HBM)
    return pl.pallas_call(
        update_kernel,
        out_shape=jax.ShapeDtypeStruct((groups, padded, cols), jnp.float32),
        in_specs=[pl.BlockSpec(memory_space=pltpu.SMEM)] + [hbm] * (7 + len(PARTS)),
        out_specs=pl.BlockSpec(memory_space=pltpu.VMEM),
        scratch_shapes=[pltpu.VMEM(v.shape, jnp.float32) for v in incoming]
        + [
            pltpu.VMEM((4, SLOTS, d, d), jnp.bfloat16),
            pltpu.VMEM((3, SLOTS, d, cols), jnp.float32),
            pltpu.VMEM((d, cols), jnp.bfloat16),
            pltpu.VMEM((d, cols), jnp.bfloat16),
            pltpu.VMEM((groups, padded, cols), jnp.float32),
            pltpu.SemaphoreType.DMA((len(PARTS),)),
            pltpu.SemaphoreType.DMA((4, SLOTS)),
            pltpu.SemaphoreType.DMA((3, SLOTS)),
        ],
        compiler_params=pltpu.CompilerParams(vmem_limit_bytes=VMEM),
        cost_estimate=pl.CostEstimate(
            flops=24 * d * d * cols, bytes_accessed=36 * d * cols, transcendentals=2 * d * cols
        ),
        name="update",
    )(chosen, *incoming, *halves, m1, m2, held)


def refresh_kernel(
    at, g0, g1, g2, g3, f0, f1, f2, f3, b_hi, b_lo, o_ref,
    g_in, f_in, gbuf, xbuf, abuf, stack, x_ref, a_ref, g_sem, f_sem, b_sem,
):
    d = x_ref.shape[0]
    w = g0.shape[1]
    kc = 4 * w
    rows = f0.shape[0]
    get_g = [pltpu.make_async_copy(r, g_in.at[k], g_sem.at[k]) for k, r in enumerate((g0, g1, g2, g3))]
    get_f = [
        pltpu.make_async_copy(r, f_in.at[pl.ds(start, rows)], f_sem.at[k])
        for k, (r, start) in enumerate(zip((f0, f1, f2, f3), row_starts(at[0], rows, 4)))
    ]
    get_b = [
        pltpu.make_async_copy(r.at[at[1]], stack.at[pl.ds(k * d, d)], b_sem.at[k])
        for k, r in enumerate((b_hi, b_hi, b_lo))
    ]
    start_all(get_g)
    start_all(get_f)
    start_all(get_b)

    def put(buf, k, v, r=0, c=0):
        hi, lo = split(v)
        n, m = v.shape
        buf[r:r + n, c:c + m] = lo
        buf[r:r + n, k + c:k + c + m] = hi
        buf[r:r + n, 2 * k + c:2 * k + c + m] = hi
        return hi, lo

    def gram(buf, k, use):
        for c in range(0, d, BLOCK):
            e = min(c + BLOCK, d)
            p = mm(buf[c:, :2 * k], buf[c:e, k:], NT) + mm(buf[c:, k:2 * k], buf[c:e, :k], NT)
            use(p, c, c)
            if e < d:
                use(p[e - c:].T, c, e)

    def times_stack():
        return mm(abuf[:, :2 * d], stack[:2 * d], NN) + mm(abuf[:, d:2 * d], stack[2 * d:], NN)

    for b in range(4):
        get_g[b].wait()
        base = 0
        for part in range(len(PARTS)):
            for source, row, size in scattered(part):
                put(gbuf, kc, g_in[b, base + source:base + source + size], row, b * w)
            base += NZ * PARTS[part]
    wait_all(get_f)

    def use_outer(v, r, c):
        n, m = v.shape
        put(abuf, d, 0.95 * f_in[r:r + n, c:c + m] + 0.05 * v, r, c)

    gram(gbuf, kc, use_outer)
    wait_all(get_b)
    power = times_stack()
    total = jnp.sum(power * power)
    x_ref[...] = power / jnp.sqrt(jnp.full((1, 1), total + 1e-06, jnp.float32))

    def step(_, carry):
        hi, lo = put(xbuf, d, x_ref[...])
        stack[:d] = hi
        stack[d:2 * d] = hi
        stack[2 * d:] = lo

        def use_inner(v, r, c):
            n, m = v.shape
            a_ref[r:r + n, c:c + m] = v
            put(abuf, d, v, r, c)

        def use_squared(v, r, c):
            n, m = v.shape
            a_ref[r:r + n, c:c + m] = -4.775 * a_ref[r:r + n, c:c + m] + 2.0315 * v

        gram(xbuf, d, use_inner)
        gram(abuf, d, use_squared)
        hi, lo = split(a_ref[...])
        abuf[:, :d] = lo
        abuf[:, d:2 * d] = hi
        x_ref[...] = 3.4445 * x_ref[...] + times_stack()
        return carry

    lax.fori_loop(0, NS_ITERS, step, 0)
    o_ref[...] = jnp.where(at[2] > 0, x_ref[...], 0.0)


def refresh(scalars, pieces, factors, b_hi, b_lo):
    d = factors[0].shape[1]
    w = pieces[0].shape[1]
    hbm = pl.BlockSpec(memory_space=pltpu.HBM)
    return pl.pallas_call(
        refresh_kernel,
        out_shape=jax.ShapeDtypeStruct((d, d), jnp.float32),
        in_specs=[pl.BlockSpec(memory_space=pltpu.SMEM)] + [hbm] * 10,
        out_specs=pl.BlockSpec(memory_space=pltpu.VMEM),
        scratch_shapes=[
            pltpu.VMEM((4, d, w), jnp.float32),
            pltpu.VMEM((d, d), jnp.float32),
            pltpu.VMEM((d, 12 * w), jnp.bfloat16),
            pltpu.VMEM((d, 3 * d), jnp.bfloat16),
            pltpu.VMEM((d, 3 * d), jnp.bfloat16),
            pltpu.VMEM((3 * d, d), jnp.bfloat16),
            pltpu.VMEM((d, d), jnp.float32),
            pltpu.VMEM((d, d), jnp.float32),
            pltpu.SemaphoreType.DMA((4,)),
            pltpu.SemaphoreType.DMA((4,)),
            pltpu.SemaphoreType.DMA((3,)),
        ],
        compiler_params=pltpu.CompilerParams(vmem_limit_bytes=VMEM),
        cost_estimate=pl.CostEstimate(
            flops=6 * 10 * d**3, bytes_accessed=16 * d * d, transcendentals=0
        ),
        name="refresh",
    )(scalars, *pieces, *factors, b_hi, b_lo)


def line(x, z, core):
    return (x * NZ + z) * NC + core


def owned_gradients(local, owner, slot, d):
    x, core = d // (NZ * NC), d % NC
    count, rows, cols = local.shape
    groups = NX * NZ * NC
    along_x = [[line(a, b, c) for a in range(NX)] for b in range(NZ) for c in range(NC)]
    along_z = [[line(a, b, c) for b in range(NZ)] for a in range(NX) for c in range(NC)]
    across = [[line(a, b, c) for a in range(NX) for c in range(NC)] for b in range(NZ)]
    swap = [
        (line(a, b, c), line(a, b, 1 - c))
        for a in range(NX) for b in range(NZ) for c in range(NC)
    ]

    def exchange(v, lines):
        return lax.all_to_all(v, "dp", 0, 0, axis_index_groups=lines, tiled=True)

    hits = (owner[None, None, :] == jnp.arange(groups)[:, None, None]) & (
        slot[None, None, :] == jnp.arange(SLOTS)[None, :, None]
    )
    matrix_of = jnp.sum(jnp.where(hits, jnp.arange(count)[None, None, :], 0), axis=2)
    wanted = lax.dynamic_index_in_dim(matrix_of.reshape(NX, NZ, NC, SLOTS), x, 0, keepdims=False)
    wanted = lax.dynamic_index_in_dim(wanted, core, 1, keepdims=False).reshape(-1)

    paired = local.reshape(NX, NC, NZ, rows // NZ, cols)
    others = lax.dynamic_index_in_dim(paired, 1 - core, 1, keepdims=False)
    kept = lax.dynamic_index_in_dim(paired, core, 1, keepdims=False)
    outs = []
    lead = 0
    for size in PARTS:
        came = lax.ppermute(
            others[:, :, lead:lead + size].astype(jnp.float32).reshape(NX, NZ * size, cols), "dp", swap
        )
        chip = kept[:, :, lead:lead + size].astype(jnp.float32).reshape(NX, NZ * size, cols) + came
        lead += size
        outs.append(exchange(chip, along_x))
    incoming = []
    for part, size in enumerate(PARTS):
        over_x = jnp.sum(outs[part], axis=0)
        over_z = jnp.sum(exchange(over_x.reshape(NZ, size, cols), along_z), axis=0)
        mean = over_z * (1.0 / groups)
        everything = exchange(jnp.broadcast_to(mean[None], (count, size, cols)), across)
        outgoing = jnp.take(everything, wanted, axis=0, mode="clip")
        incoming.append(exchange(outgoing.reshape(NZ, SLOTS, size, cols), along_z))
    return incoming


def body(partials, owner, rowblock, factor, basis, moment1, moment2, master):
    groups = lax.axis_size("dp")
    cols = lax.axis_size("mp")
    d = lax.axis_index("dp")
    y = lax.axis_index("mp")
    core = d % NC
    count = owner.shape[0]
    rows = factor.shape[1]
    order = jnp.arange(count)
    same = owner[:, None] == owner[None, :]
    slot = jnp.sum((same & (order[None, :] < order[:, None])).astype(jnp.int32), axis=1)
    mine = (owner[None, :] == d) & (slot[None, :] == jnp.arange(SLOTS)[:, None])
    valid = jnp.any(mine, axis=1)
    my_matrix = jnp.sum(jnp.where(mine, order[None, :], 0), axis=1)

    everyone = [(g, j) for g in range(groups) for j in range(cols)]

    def ring(shift, parity):
        return [
            (g * cols + j, g * cols + (j + shift) % cols)
            for g, j in everyone
            if parity is None or (j - g) % 2 == parity
        ]

    def move(v, shift, parity=None):
        return lax.ppermute(v, ("dp", "mp"), ring(shift, parity))

    def target_slot(at):
        return ((at - core) % cols) // 2

    even = (y - core) % 2 == 0
    own_slot = target_slot(y)
    left_slot = target_slot(y - 1)

    def to_targets(pick):
        return (
            pick(own_slot),
            move(pick(left_slot), -1, 1),
            move(pick(1 - own_slot), 2, 0),
            move(pick(1 - left_slot), 1, 1),
        )

    keep = jnp.where(own_slot == 0, valid[0], valid[1])
    scalars = jnp.stack([y, own_slot, keep.astype(jnp.int32)]).astype(jnp.int32)
    basis_rows = jnp.concatenate([basis[0, :, 0], basis[0, :, 1]], axis=1)
    blocks = (basis_rows, move(basis_rows, -1), move(basis_rows, 2), move(basis_rows, 1))
    halves = prepare(scalars, blocks)
    factors = to_targets(lambda s: jnp.where(s == 0, factor[0, :, 0], factor[0, :, 1]))

    incoming = owned_gradients(partials[0], owner, slot, d)

    def block_of(s):
        return jnp.concatenate(
            [
                jnp.where(s == 0, v[:, 0], v[:, 1]).reshape(-1, v.shape[-1])
                for v in incoming
            ],
            axis=0,
        )

    pieces = to_targets(block_of)
    chosen = jnp.sum(jnp.where(mine[:, :, None], rowblock[None], 0), axis=1)
    sent = update(chosen, incoming, halves, moment1[0], moment2[0], master[0])
    received = lax.all_to_all(sent, "dp", split_axis=0, concat_axis=0, tiled=True)
    refreshed = refresh(scalars, pieces, factors, halves[0], halves[1])

    landed = jnp.take(received, owner, axis=0, mode="clip")
    block_rows = rows * cols // groups
    train_weights = jnp.where(
        (slot == 0)[:, None, None], landed[:, :block_rows], landed[:, block_rows:2 * block_rows]
    )[:, None]

    def row_block(at):
        return lax.dynamic_slice_in_dim(refreshed, ((at + cols) % cols) * rows, rows, 0)

    own = row_block(y)
    from_left = move(row_block(y + 1), 1, 0)
    from_far = move(row_block(y + 2), 2, 0)
    from_right = move(row_block(y - 1), -1, 0)
    near = jnp.where(even, own, from_left)
    far = jnp.where(even, from_far, from_right)
    near_first = jnp.where(even, own_slot, left_slot) == 0
    new_basis = jnp.stack(
        [jnp.where(near_first, near, far), jnp.where(near_first, far, near)], axis=1
    )
    return (train_weights, new_basis[None])


def solution(mesh):
    placed = (
        P("dp", None, None, "mp"),
        P(),
        P(),
        P("dp", "mp", None, None),
        P("dp", "mp", None, None),
        P("dp", None, None, "mp"),
        P("dp", None, None, "mp"),
        P("dp", None, None, "mp"),
    )

    return jax.shard_map(
        body,
        mesh=mesh,
        in_specs=placed,
        out_specs=(P(None, "dp", None, "mp"), P("dp", "mp", None, None)),
        check_vma=False,
    )
```

```python
import jax
import jax.numpy as jnp
from jax import lax
from jax.experimental import pallas as pl
from jax.experimental.pallas import tpu as pltpu
from jax.sharding import PartitionSpec as P


NS_ITERS = 4
SLOTS = 2
BLOCK = 256
FIRST = 64
VMEM = 63 << 20
PARTS = (80,)
NX, NZ, NC = 4, 8, 2
NT = (((1,), (1,)), ((), ()))
NN = (((1,), (0,)), ((), ()))


def split(x):
    hi = x.astype(jnp.bfloat16)
    lo = (x - hi.astype(jnp.float32)).astype(jnp.bfloat16)
    return hi, lo


def mm(left, right, dims):
    return lax.dot_general(left, right, dims, preferred_element_type=jnp.float32)


def mm3(left, right, dims=NN):
    (lh, ll), (rh, rl) = left, right
    return mm(lh, rh, dims) + (mm(lh, rl, dims) + mm(ll, rh, dims))


def row_starts(y, rows, cols):
    return [pl.multiple_of(lax.rem(y + k, cols) * rows, 32) for k in range(cols)]


def scattered(part):
    lead = sum(PARTS[:part])
    whole = sum(PARTS)
    return [(z * PARTS[part], z * whole + lead, PARTS[part]) for z in range(NZ)]


def start_all(copies):
    for copy in copies:
        copy.start()


def wait_all(copies):
    for copy in copies:
        copy.wait()


def prepare_kernel(at, b0, b1, b2, b3, hi_ref, lo_ref, thi_ref, tlo_ref, held, whole, parts, in_sem, out_sem):
    blocks = (b0, b1, b2, b3)
    rows, d = b0.shape[0], whole.shape[0]
    fetch = [pltpu.make_async_copy(b, held.at[k], in_sem.at[k]) for k, b in enumerate(blocks)]
    start_all(fetch)
    wait_all(fetch)
    starts = row_starts(at[0], rows, len(blocks))
    stores = []
    for s in range(SLOTS):
        for k, start in enumerate(starts):
            whole[pl.ds(start, rows), :] = held[k, :, s * d:(s + 1) * d]
        b = whole[...]
        parts[0, s], parts[1, s] = split(b)
        parts[2, s], parts[3, s] = split(b.T)
        mine = [
            pltpu.make_async_copy(parts.at[k, s], ref.at[s], out_sem.at[k, s])
            for k, ref in enumerate((hi_ref, lo_ref, thi_ref, tlo_ref))
        ]
        start_all(mine)
        stores += mine
    wait_all(stores)


def prepare(scalars, blocks):
    rows, wide = blocks[0].shape
    d = wide // SLOTS
    half = jax.ShapeDtypeStruct((SLOTS, d, d), jnp.bfloat16)
    hbm = pl.BlockSpec(memory_space=pltpu.HBM)
    return pl.pallas_call(
        prepare_kernel,
        out_shape=[half] * 4,
        in_specs=[pl.BlockSpec(memory_space=pltpu.SMEM)] + [hbm] * 4,
        out_specs=[hbm] * 4,
        scratch_shapes=[
            pltpu.VMEM((4, rows, wide), jnp.float32),
            pltpu.VMEM((d, d), jnp.float32),
            pltpu.VMEM((4, SLOTS, d, d), jnp.bfloat16),
            pltpu.SemaphoreType.DMA((4,)),
            pltpu.SemaphoreType.DMA((4, SLOTS)),
        ],
        compiler_params=pltpu.CompilerParams(vmem_limit_bytes=VMEM),
        cost_estimate=pl.CostEstimate(flops=8 * d * d, bytes_accessed=24 * d * d, transcendentals=0),
        name="prepare",
    )(scalars, *blocks)


def update_kernel(chosen, *refs):
    count = len(PARTS)
    incoming, sources, states, out = refs[:count], refs[count:count + 4], refs[count + 4:count + 7], refs[count + 7]
    scratch = refs[count + 8:]
    came, (parts, state, gh, gl, weights, came_sem, part_sem, state_sem) = scratch[:count], scratch[count:]
    groups = out.shape[0]
    block = state.shape[2] // groups
    order = (2, 3, 0, 1)
    get_came = [pltpu.make_async_copy(r, c, came_sem.at[k]) for k, (r, c) in enumerate(zip(incoming, came))]
    get_part = [
        [pltpu.make_async_copy(sources[k].at[s], parts.at[k, s], part_sem.at[k, s]) for k in order]
        for s in range(SLOTS)
    ]
    get_state = [
        [pltpu.make_async_copy(r.at[s], state.at[k, s], state_sem.at[k, s]) for k, r in enumerate(states)]
        for s in range(SLOTS)
    ]
    start_all(get_came)
    for s in range(SLOTS):
        start_all(get_part[s])
        start_all(get_state[s])
    wait_all(get_came)
    for s in range(SLOTS):
        for part, ref in enumerate(came):
            for z, (_, row, size) in enumerate(scattered(part)):
                gh[row:row + size], gl[row:row + size] = split(ref[z, s])
        wait_all(get_part[s][:2])
        turned = mm3((parts[2, s], parts[3, s]), (gh[...], gl[...]))
        wait_all(get_state[s])
        first = 0.9 * state[0, s] + 0.1 * turned
        second = 0.95 * state[1, s] + 0.05 * turned * turned
        wait_all(get_part[s][2:])
        direction = mm3((parts[0, s], parts[1, s]), split(first / (jnp.sqrt(second) + 1e-08)))
        fresh = state[2, s] - 0.1 * (direction + 0.1 * state[2, s])
        here = slice(s * block, (s + 1) * block)
        for j in range(groups):
            weights[j, here, :] = fresh[j * block:(j + 1) * block]

        def send(j, carry):
            out[j, here, :] = weights[chosen[s, j], here, :]
            return carry

        lax.fori_loop(0, groups, send, 0, unroll=4)


def update(chosen, incoming, halves, m1, m2, held):
    groups = chosen.shape[1]
    d, cols = m1.shape[1:]
    block = d // groups
    padded = -(-SLOTS * block // 8) * 8
    hbm = pl.BlockSpec(memory_space=pltpu.HBM)
    return pl.pallas_call(
        update_kernel,
        out_shape=jax.ShapeDtypeStruct((groups, padded, cols), jnp.float32),
        in_specs=[pl.BlockSpec(memory_space=pltpu.SMEM)] + [hbm] * (7 + len(PARTS)),
        out_specs=pl.BlockSpec(memory_space=pltpu.VMEM),
        scratch_shapes=[pltpu.VMEM(v.shape, jnp.float32) for v in incoming]
        + [
            pltpu.VMEM((4, SLOTS, d, d), jnp.bfloat16),
            pltpu.VMEM((3, SLOTS, d, cols), jnp.float32),
            pltpu.VMEM((d, cols), jnp.bfloat16),
            pltpu.VMEM((d, cols), jnp.bfloat16),
            pltpu.VMEM((groups, padded, cols), jnp.float32),
            pltpu.SemaphoreType.DMA((len(PARTS),)),
            pltpu.SemaphoreType.DMA((4, SLOTS)),
            pltpu.SemaphoreType.DMA((3, SLOTS)),
        ],
        compiler_params=pltpu.CompilerParams(vmem_limit_bytes=VMEM),
        cost_estimate=pl.CostEstimate(
            flops=24 * d * d * cols, bytes_accessed=36 * d * cols, transcendentals=2 * d * cols
        ),
        name="update",
    )(chosen, *incoming, *halves, m1, m2, held)


def refresh_kernel(
    at, g0, g1, g2, g3, f0, f1, f2, f3, b_hi, b_lo, o0, o1, o2, o3,
    g_in, f_in, gbuf, xbuf, abuf, stack, x_ref, a_ref, g_sem, f_sem, b_sem,
):
    d = x_ref.shape[0]
    w = g0.shape[1]
    kc = 4 * w
    rows = f0.shape[0]
    get_g = [pltpu.make_async_copy(r, g_in.at[k], g_sem.at[k]) for k, r in enumerate((g0, g1, g2, g3))]
    get_f = [
        pltpu.make_async_copy(r, f_in.at[pl.ds(start, rows)], f_sem.at[k])
        for k, (r, start) in enumerate(zip((f0, f1, f2, f3), row_starts(at[0], rows, 4)))
    ]
    get_b = [
        pltpu.make_async_copy(r.at[at[1]], stack.at[pl.ds(k * d, d)], b_sem.at[k])
        for k, r in enumerate((b_hi, b_hi, b_lo))
    ]
    start_all(get_g)
    start_all(get_f)
    start_all(get_b)

    def put(buf, k, v, r=0, c=0):
        hi, lo = split(v)
        n, m = v.shape
        buf[r:r + n, c:c + m] = lo
        buf[r:r + n, k + c:k + c + m] = hi
        buf[r:r + n, 2 * k + c:2 * k + c + m] = hi
        return hi, lo

    def gram(buf, k, use):
        for c in range(0, d, BLOCK):
            e = min(c + BLOCK, d)
            p = mm(buf[c:, :2 * k], buf[c:e, k:], NT) + mm(buf[c:, k:2 * k], buf[c:e, :k], NT)
            use(p, c, c)
            if e < d:
                use(p[e - c:].T, c, e)

    def times_stack():
        return mm(abuf[:, :2 * d], stack[:2 * d], NN) + mm(abuf[:, d:2 * d], stack[2 * d:], NN)

    for b in range(4):
        get_g[b].wait()
        base = 0
        for part in range(len(PARTS)):
            for source, row, size in scattered(part):
                put(gbuf, kc, g_in[b, base + source:base + source + size], row, b * w)
            base += NZ * PARTS[part]
    wait_all(get_f)

    def use_outer(v, r, c):
        n, m = v.shape
        put(abuf, d, 0.95 * f_in[r:r + n, c:c + m] + 0.05 * v, r, c)

    gram(gbuf, kc, use_outer)
    wait_all(get_b)
    power = times_stack()
    total = jnp.sum(power * power)
    x_ref[...] = power / jnp.sqrt(jnp.full((1, 1), total + 1e-06, jnp.float32))

    def step(_, carry):
        hi, lo = put(xbuf, d, x_ref[...])
        stack[:d] = hi
        stack[d:2 * d] = hi
        stack[2 * d:] = lo

        def use_inner(v, r, c):
            n, m = v.shape
            a_ref[r:r + n, c:c + m] = v
            put(abuf, d, v, r, c)

        def use_squared(v, r, c):
            n, m = v.shape
            a_ref[r:r + n, c:c + m] = -4.775 * a_ref[r:r + n, c:c + m] + 2.0315 * v

        gram(xbuf, d, use_inner)
        gram(abuf, d, use_squared)
        hi, lo = split(a_ref[...])
        abuf[:, :d] = lo
        abuf[:, d:2 * d] = hi
        x_ref[...] = 3.4445 * x_ref[...] + times_stack()
        return carry

    lax.fori_loop(0, NS_ITERS, step, 0)
    for start, o_ref in zip(row_starts(at[0], rows, 4), (o0, o1, o2, o3)):
        o_ref[...] = jnp.where(at[2] > 0, x_ref[pl.ds(start, rows), :], 0.0)


def refresh(scalars, pieces, factors, b_hi, b_lo):
    d = factors[0].shape[1]
    w = pieces[0].shape[1]
    hbm = pl.BlockSpec(memory_space=pltpu.HBM)
    return pl.pallas_call(
        refresh_kernel,
        out_shape=[jax.ShapeDtypeStruct(factors[0].shape, jnp.float32)] * 4,
        in_specs=[pl.BlockSpec(memory_space=pltpu.SMEM)] + [hbm] * 10,
        out_specs=[pl.BlockSpec(memory_space=pltpu.VMEM)] * 4,
        scratch_shapes=[
            pltpu.VMEM((4, d, w), jnp.float32),
            pltpu.VMEM((d, d), jnp.float32),
            pltpu.VMEM((d, 12 * w), jnp.bfloat16),
            pltpu.VMEM((d, 3 * d), jnp.bfloat16),
            pltpu.VMEM((d, 3 * d), jnp.bfloat16),
            pltpu.VMEM((3 * d, d), jnp.bfloat16),
            pltpu.VMEM((d, d), jnp.float32),
            pltpu.VMEM((d, d), jnp.float32),
            pltpu.SemaphoreType.DMA((4,)),
            pltpu.SemaphoreType.DMA((4,)),
            pltpu.SemaphoreType.DMA((3,)),
        ],
        compiler_params=pltpu.CompilerParams(vmem_limit_bytes=VMEM),
        cost_estimate=pl.CostEstimate(
            flops=6 * 10 * d**3, bytes_accessed=16 * d * d, transcendentals=0
        ),
        name="refresh",
    )(scalars, *pieces, *factors, b_hi, b_lo)


def line(x, z, core):
    return (x * NZ + z) * NC + core


def owned_gradients(local, owner, slot, d):
    x, core = d // (NZ * NC), d % NC
    count, rows, cols = local.shape
    groups = NX * NZ * NC
    along_z = [[line(a, b, c) for b in range(NZ)] for a in range(NX) for c in range(NC)]
    across = [[line(a, b, c) for a in range(NX) for c in range(NC)] for b in range(NZ)]
    swap = [
        (line(a, b, c), line(a, b, 1 - c))
        for a in range(NX) for b in range(NZ) for c in range(NC)
    ]

    def exchange(v, lines):
        return lax.all_to_all(v, "dp", 0, 0, axis_index_groups=lines, tiled=True)

    hits = (owner[None, None, :] == jnp.arange(groups)[:, None, None]) & (
        slot[None, None, :] == jnp.arange(SLOTS)[None, :, None]
    )
    matrix_of = jnp.sum(jnp.where(hits, jnp.arange(count)[None, None, :], 0), axis=2)
    wanted = lax.dynamic_index_in_dim(matrix_of.reshape(NX, NZ, NC, SLOTS), x, 0, keepdims=False)
    wanted = lax.dynamic_index_in_dim(wanted, core, 1, keepdims=False).reshape(-1)

    def along(shift):
        return [
            (line(a, b, c), line((a + shift) % NX, b, c))
            for a in range(NX) for b in range(NZ) for c in range(NC)
        ]

    part = rows // NZ
    rest = part - FIRST
    paired = local.reshape(NX, NC, NZ, part, cols)
    others = lax.dynamic_index_in_dim(paired, 1 - core, 1, keepdims=False)
    kept = lax.dynamic_index_in_dim(paired, core, 1, keepdims=False)
    came = lax.ppermute(others.astype(jnp.float32), "dp", swap)
    chip = kept.astype(jnp.float32) + came

    def towards(shift):
        near = lax.dynamic_index_in_dim(chip, (x + shift) % NX, 0, keepdims=False)
        return near[:, :FIRST].reshape(NZ * FIRST, cols)

    cut = NZ * FIRST // 2
    far = towards(2)
    far_up = lax.ppermute(far[:cut], "dp", along(1))
    far_down = lax.ppermute(far[cut:], "dp", along(-1))
    late = jnp.transpose(chip[:, :, FIRST:], (1, 0, 2, 3)).reshape(NZ, NX * rest, cols)
    late = exchange(late, along_z)
    up, down = towards(1), towards(3)
    up = jnp.concatenate([up[:cut] + far_up, up[cut:]], axis=0)
    down = jnp.concatenate([down[:cut], down[cut:] + far_down], axis=0)
    from_up = lax.ppermute(up, "dp", along(1))
    from_down = lax.ppermute(down, "dp", along(-1))
    over_x = towards(0) + from_up + from_down
    over_z = jnp.sum(exchange(over_x.reshape(NZ, FIRST, cols), along_z), axis=0)
    mean = over_z * (1.0 / groups)
    late = jnp.sum(late, axis=0)
    late = (late + lax.ppermute(late, "dp", along(1))) + (
        lax.ppermute(late, "dp", along(-1)) + lax.ppermute(late, "dp", along(2))
    )
    late = (late * (1.0 / groups)).reshape(NX, rest, cols)
    other = lax.ppermute(late, "dp", swap)
    late = jnp.stack(
        [jnp.where(core == 0, late, other), jnp.where(core == 0, other, late)], axis=1
    ).reshape(count, rest, cols)
    everything = exchange(jnp.broadcast_to(mean[None], (count, FIRST, cols)), across)
    everything = jnp.concatenate([everything, late], axis=1)
    outgoing = jnp.take(everything, wanted, axis=0, mode="clip")
    return [exchange(outgoing.reshape(NZ, SLOTS, part, cols), along_z)]


def body(partials, owner, rowblock, factor, basis, moment1, moment2, master):
    groups = lax.axis_size("dp")
    cols = lax.axis_size("mp")
    d = lax.axis_index("dp")
    y = lax.axis_index("mp")
    core = d % NC
    count = owner.shape[0]
    rows = factor.shape[1]
    order = jnp.arange(count)
    same = owner[:, None] == owner[None, :]
    slot = jnp.sum((same & (order[None, :] < order[:, None])).astype(jnp.int32), axis=1)
    mine = (owner[None, :] == d) & (slot[None, :] == jnp.arange(SLOTS)[:, None])
    valid = jnp.any(mine, axis=1)
    my_matrix = jnp.sum(jnp.where(mine, order[None, :], 0), axis=1)

    everyone = [(g, j) for g in range(groups) for j in range(cols)]

    def ring(shift, parity):
        return [
            (g * cols + j, g * cols + (j + shift) % cols)
            for g, j in everyone
            if parity is None or (j - g) % 2 == parity
        ]

    def move(v, shift, parity=None):
        return lax.ppermute(v, ("dp", "mp"), ring(shift, parity))

    def target_slot(at):
        return ((at - core) % cols) // 2

    even = (y - core) % 2 == 0
    own_slot = target_slot(y)
    left_slot = target_slot(y - 1)

    def to_targets(pick):
        return (
            pick(own_slot),
            move(pick(left_slot), -1, 1),
            move(pick(1 - own_slot), 2, 0),
            move(pick(1 - left_slot), 1, 1),
        )

    keep = jnp.where(own_slot == 0, valid[0], valid[1])
    scalars = jnp.stack([y, own_slot, keep.astype(jnp.int32)]).astype(jnp.int32)
    basis_rows = jnp.concatenate([basis[0, :, 0], basis[0, :, 1]], axis=1)
    blocks = (basis_rows, move(basis_rows, -1), move(basis_rows, 2), move(basis_rows, 1))
    halves = prepare(scalars, blocks)
    factors = to_targets(lambda s: jnp.where(s == 0, factor[0, :, 0], factor[0, :, 1]))

    incoming = owned_gradients(partials[0], owner, slot, d)

    def block_of(s):
        return jnp.concatenate(
            [
                jnp.where(s == 0, v[:, 0], v[:, 1]).reshape(-1, v.shape[-1])
                for v in incoming
            ],
            axis=0,
        )

    pieces = to_targets(block_of)
    chosen = jnp.sum(jnp.where(mine[:, :, None], rowblock[None], 0), axis=1)
    sent = update(chosen, incoming, halves, moment1[0], moment2[0], master[0])
    received = lax.all_to_all(sent, "dp", split_axis=0, concat_axis=0, tiled=True)
    own, after, across, before = refresh(scalars, pieces, factors, halves[0], halves[1])

    landed = jnp.take(received, owner, axis=0, mode="clip")
    block_rows = rows * cols // groups
    train_weights = jnp.where(
        (slot == 0)[:, None, None], landed[:, :block_rows], landed[:, block_rows:2 * block_rows]
    )[:, None]

    from_left = move(after, 1, 0)
    from_far = move(across, 2, 0)
    from_right = move(before, -1, 0)
    near = jnp.where(even, own, from_left)
    far = jnp.where(even, from_far, from_right)
    near_first = jnp.where(even, own_slot, left_slot) == 0
    new_basis = jnp.stack(
        [jnp.where(near_first, near, far), jnp.where(near_first, far, near)], axis=1
    )
    return (train_weights, new_basis[None])


def solution(mesh):
    placed = (
        P("dp", None, None, "mp"),
        P(),
        P(),
        P("dp", "mp", None, None),
        P("dp", "mp", None, None),
        P("dp", None, None, "mp"),
        P("dp", None, None, "mp"),
        P("dp", None, None, "mp"),
    )

    return jax.shard_map(
        body,
        mesh=mesh,
        in_specs=placed,
        out_specs=(P(None, "dp", None, "mp"), P("dp", "mp", None, None)),
        check_vma=False,
    )
```

```python
import jax
import jax.numpy as jnp
from jax import lax
from jax.experimental import pallas as pl
from jax.experimental.pallas import tpu as pltpu
from jax.sharding import PartitionSpec as P


NS_ITERS = 4
SLOTS = 2
BLOCK = 256
FIRST = 64
VMEM = 63 << 20
PARTS = (80,)
NX, NZ, NC = 4, 8, 2
NT = (((1,), (1,)), ((), ()))
NN = (((1,), (0,)), ((), ()))


def split(x):
    hi = x.astype(jnp.bfloat16)
    lo = (x - hi.astype(jnp.float32)).astype(jnp.bfloat16)
    return hi, lo


def mm(left, right, dims):
    return lax.dot_general(left, right, dims, preferred_element_type=jnp.float32)


def mm3(left, right, dims=NN):
    (lh, ll), (rh, rl) = left, right
    return mm(lh, rh, dims) + (mm(lh, rl, dims) + mm(ll, rh, dims))


def row_starts(y, rows, cols):
    return [pl.multiple_of(lax.rem(y + k, cols) * rows, 32) for k in range(cols)]


def scattered(part):
    lead = sum(PARTS[:part])
    whole = sum(PARTS)
    return [(z * PARTS[part], z * whole + lead, PARTS[part]) for z in range(NZ)]


def start_all(copies):
    for copy in copies:
        copy.start()


def wait_all(copies):
    for copy in copies:
        copy.wait()


def prepare_kernel(at, b0, b1, b2, b3, hi_ref, lo_ref, thi_ref, tlo_ref, held, whole, parts, in_sem, out_sem):
    blocks = (b0, b1, b2, b3)
    rows, d = b0.shape[0], whole.shape[0]
    fetch = [pltpu.make_async_copy(b, held.at[k], in_sem.at[k]) for k, b in enumerate(blocks)]
    start_all(fetch)
    wait_all(fetch)
    starts = row_starts(at[0], rows, len(blocks))
    stores = []
    for s in range(SLOTS):
        for k, start in enumerate(starts):
            whole[pl.ds(start, rows), :] = held[k, :, s * d:(s + 1) * d]
        b = whole[...]
        parts[0, s], parts[1, s] = split(b)
        parts[2, s], parts[3, s] = split(b.T)
        mine = [
            pltpu.make_async_copy(parts.at[k, s], ref.at[s], out_sem.at[k, s])
            for k, ref in enumerate((hi_ref, lo_ref, thi_ref, tlo_ref))
        ]
        start_all(mine)
        stores += mine
    wait_all(stores)


def prepare(scalars, blocks):
    rows, wide = blocks[0].shape
    d = wide // SLOTS
    half = jax.ShapeDtypeStruct((SLOTS, d, d), jnp.bfloat16)
    hbm = pl.BlockSpec(memory_space=pltpu.HBM)
    return pl.pallas_call(
        prepare_kernel,
        out_shape=[half] * 4,
        in_specs=[pl.BlockSpec(memory_space=pltpu.SMEM)] + [hbm] * 4,
        out_specs=[hbm] * 4,
        scratch_shapes=[
            pltpu.VMEM((4, rows, wide), jnp.float32),
            pltpu.VMEM((d, d), jnp.float32),
            pltpu.VMEM((4, SLOTS, d, d), jnp.bfloat16),
            pltpu.SemaphoreType.DMA((4,)),
            pltpu.SemaphoreType.DMA((4, SLOTS)),
        ],
        compiler_params=pltpu.CompilerParams(vmem_limit_bytes=VMEM),
        cost_estimate=pl.CostEstimate(flops=8 * d * d, bytes_accessed=24 * d * d, transcendentals=0),
        name="prepare",
    )(scalars, *blocks)


def update_kernel(chosen, *refs):
    count = len(PARTS)
    incoming, sources, states, out = refs[:count], refs[count:count + 4], refs[count + 4:count + 7], refs[count + 7]
    scratch = refs[count + 8:]
    came, (parts, state, gh, gl, weights, came_sem, part_sem, state_sem) = scratch[:count], scratch[count:]
    groups = out.shape[0]
    block = state.shape[2] // groups
    order = (2, 3, 0, 1)
    get_came = [pltpu.make_async_copy(r, c, came_sem.at[k]) for k, (r, c) in enumerate(zip(incoming, came))]
    get_part = [
        [pltpu.make_async_copy(sources[k].at[s], parts.at[k, s], part_sem.at[k, s]) for k in order]
        for s in range(SLOTS)
    ]
    get_state = [
        [pltpu.make_async_copy(r.at[s], state.at[k, s], state_sem.at[k, s]) for k, r in enumerate(states)]
        for s in range(SLOTS)
    ]
    start_all(get_came)
    for s in range(SLOTS):
        start_all(get_part[s])
        start_all(get_state[s])
    wait_all(get_came)
    for s in range(SLOTS):
        for part, ref in enumerate(came):
            for z, (_, row, size) in enumerate(scattered(part)):
                gh[row:row + size], gl[row:row + size] = split(ref[z, s])
        wait_all(get_part[s][:2])
        turned = mm3((parts[2, s], parts[3, s]), (gh[...], gl[...]))
        wait_all(get_state[s])
        first = 0.9 * state[0, s] + 0.1 * turned
        second = 0.95 * state[1, s] + 0.05 * turned * turned
        wait_all(get_part[s][2:])
        direction = mm3((parts[0, s], parts[1, s]), split(first / (jnp.sqrt(second) + 1e-08)))
        fresh = state[2, s] - 0.1 * (direction + 0.1 * state[2, s])
        here = slice(s * block, (s + 1) * block)
        for j in range(groups):
            weights[j, here, :] = fresh[j * block:(j + 1) * block]

        def send(j, carry):
            out[j, here, :] = weights[chosen[s, j], here, :]
            return carry

        lax.fori_loop(0, groups, send, 0, unroll=4)


def update(chosen, incoming, halves, m1, m2, held):
    groups = chosen.shape[1]
    d, cols = m1.shape[1:]
    block = d // groups
    padded = -(-SLOTS * block // 8) * 8
    hbm = pl.BlockSpec(memory_space=pltpu.HBM)
    return pl.pallas_call(
        update_kernel,
        out_shape=jax.ShapeDtypeStruct((groups, padded, cols), jnp.float32),
        in_specs=[pl.BlockSpec(memory_space=pltpu.SMEM)] + [hbm] * (7 + len(PARTS)),
        out_specs=pl.BlockSpec(memory_space=pltpu.VMEM),
        scratch_shapes=[pltpu.VMEM(v.shape, jnp.float32) for v in incoming]
        + [
            pltpu.VMEM((4, SLOTS, d, d), jnp.bfloat16),
            pltpu.VMEM((3, SLOTS, d, cols), jnp.float32),
            pltpu.VMEM((d, cols), jnp.bfloat16),
            pltpu.VMEM((d, cols), jnp.bfloat16),
            pltpu.VMEM((groups, padded, cols), jnp.float32),
            pltpu.SemaphoreType.DMA((len(PARTS),)),
            pltpu.SemaphoreType.DMA((4, SLOTS)),
            pltpu.SemaphoreType.DMA((3, SLOTS)),
        ],
        compiler_params=pltpu.CompilerParams(vmem_limit_bytes=VMEM),
        cost_estimate=pl.CostEstimate(
            flops=24 * d * d * cols, bytes_accessed=36 * d * cols, transcendentals=2 * d * cols
        ),
        name="update",
    )(chosen, *incoming, *halves, m1, m2, held)


def refresh_kernel(
    at, g0, g1, g2, g3, f0, f1, f2, f3, b_hi, b_lo, o0, o1, o2, o3,
    g_in, f_in, gbuf, xbuf, abuf, stack, x_ref, a_ref, g_sem, f_sem, b_sem,
):
    d = x_ref.shape[0]
    w = g0.shape[1]
    kc = 4 * w
    rows = f0.shape[0]
    get_g = [pltpu.make_async_copy(r, g_in.at[k], g_sem.at[k]) for k, r in enumerate((g0, g1, g2, g3))]
    get_f = [
        pltpu.make_async_copy(r, f_in.at[pl.ds(start, rows)], f_sem.at[k])
        for k, (r, start) in enumerate(zip((f0, f1, f2, f3), row_starts(at[0], rows, 4)))
    ]
    get_b = [
        pltpu.make_async_copy(r.at[at[1]], stack.at[pl.ds(k * d, d)], b_sem.at[k])
        for k, r in enumerate((b_hi, b_hi, b_lo))
    ]
    start_all(get_g)
    start_all(get_f)
    start_all(get_b)

    def put(buf, k, v, r=0, c=0):
        hi, lo = split(v)
        n, m = v.shape
        buf[r:r + n, c:c + m] = lo
        buf[r:r + n, k + c:k + c + m] = hi
        buf[r:r + n, 2 * k + c:2 * k + c + m] = hi
        return hi, lo

    def gram(buf, k, use):
        for c in range(0, d, BLOCK):
            e = min(c + BLOCK, d)
            p = mm(buf[c:, :2 * k], buf[c:e, k:], NT) + mm(buf[c:, k:2 * k], buf[c:e, :k], NT)
            use(p, c, c)
            if e < d:
                use(p[e - c:].T, c, e)

    def times_stack():
        return mm(abuf[:, :2 * d], stack[:2 * d], NN) + mm(abuf[:, d:2 * d], stack[2 * d:], NN)

    for b in range(4):
        get_g[b].wait()
        base = 0
        for part in range(len(PARTS)):
            for source, row, size in scattered(part):
                put(gbuf, kc, g_in[b, base + source:base + source + size], row, b * w)
            base += NZ * PARTS[part]
    wait_all(get_f)

    def use_outer(v, r, c):
        n, m = v.shape
        put(abuf, d, 0.95 * f_in[r:r + n, c:c + m] + 0.05 * v, r, c)

    gram(gbuf, kc, use_outer)
    wait_all(get_b)
    power = times_stack()
    total = jnp.sum(power * power)
    x_ref[...] = power / jnp.sqrt(jnp.full((1, 1), total + 1e-06, jnp.float32))

    def step(_, carry):
        hi, lo = put(xbuf, d, x_ref[...])
        stack[:d] = hi
        stack[d:2 * d] = hi
        stack[2 * d:] = lo

        def use_inner(v, r, c):
            n, m = v.shape
            a_ref[r:r + n, c:c + m] = v
            put(abuf, d, v, r, c)

        def use_squared(v, r, c):
            n, m = v.shape
            a_ref[r:r + n, c:c + m] = -4.775 * a_ref[r:r + n, c:c + m] + 2.0315 * v

        gram(xbuf, d, use_inner)
        gram(abuf, d, use_squared)
        hi, lo = split(a_ref[...])
        abuf[:, :d] = lo
        abuf[:, d:2 * d] = hi
        x_ref[...] = 3.4445 * x_ref[...] + times_stack()
        return carry

    lax.fori_loop(0, NS_ITERS, step, 0)
    for start, o_ref in zip(row_starts(at[0], rows, 4), (o0, o1, o2, o3)):
        o_ref[...] = jnp.where(at[2] > 0, x_ref[pl.ds(start, rows), :], 0.0)


def refresh(scalars, pieces, factors, b_hi, b_lo):
    d = factors[0].shape[1]
    w = pieces[0].shape[1]
    hbm = pl.BlockSpec(memory_space=pltpu.HBM)
    return pl.pallas_call(
        refresh_kernel,
        out_shape=[jax.ShapeDtypeStruct(factors[0].shape, jnp.float32)] * 4,
        in_specs=[pl.BlockSpec(memory_space=pltpu.SMEM)] + [hbm] * 10,
        out_specs=[pl.BlockSpec(memory_space=pltpu.VMEM)] * 4,
        scratch_shapes=[
            pltpu.VMEM((4, d, w), jnp.float32),
            pltpu.VMEM((d, d), jnp.float32),
            pltpu.VMEM((d, 12 * w), jnp.bfloat16),
            pltpu.VMEM((d, 3 * d), jnp.bfloat16),
            pltpu.VMEM((d, 3 * d), jnp.bfloat16),
            pltpu.VMEM((3 * d, d), jnp.bfloat16),
            pltpu.VMEM((d, d), jnp.float32),
            pltpu.VMEM((d, d), jnp.float32),
            pltpu.SemaphoreType.DMA((4,)),
            pltpu.SemaphoreType.DMA((4,)),
            pltpu.SemaphoreType.DMA((3,)),
        ],
        compiler_params=pltpu.CompilerParams(vmem_limit_bytes=44 << 20),
        cost_estimate=pl.CostEstimate(
            flops=6 * 10 * d**3, bytes_accessed=16 * d * d, transcendentals=0
        ),
        name="refresh",
    )(scalars, *(pltpu.with_memory_space_constraint(v, pltpu.HBM) for v in (*pieces, *factors, b_hi, b_lo)))


def line(x, z, core):
    return (x * NZ + z) * NC + core


def owned_gradients(local, owner, slot, d):
    x, core = d // (NZ * NC), d % NC
    count, rows, cols = local.shape
    groups = NX * NZ * NC
    along_z = [[line(a, b, c) for b in range(NZ)] for a in range(NX) for c in range(NC)]
    across = [[line(a, b, c) for a in range(NX) for c in range(NC)] for b in range(NZ)]
    swap = [
        (line(a, b, c), line(a, b, 1 - c))
        for a in range(NX) for b in range(NZ) for c in range(NC)
    ]

    def exchange(v, lines):
        return lax.all_to_all(v, "dp", 0, 0, axis_index_groups=lines, tiled=True)

    hits = (owner[None, None, :] == jnp.arange(groups)[:, None, None]) & (
        slot[None, None, :] == jnp.arange(SLOTS)[None, :, None]
    )
    matrix_of = jnp.sum(jnp.where(hits, jnp.arange(count)[None, None, :], 0), axis=2)
    wanted = lax.dynamic_index_in_dim(matrix_of.reshape(NX, NZ, NC, SLOTS), x, 0, keepdims=False)
    wanted = lax.dynamic_index_in_dim(wanted, core, 1, keepdims=False).reshape(-1)

    def along(shift):
        return [
            (line(a, b, c), line((a + shift) % NX, b, c))
            for a in range(NX) for b in range(NZ) for c in range(NC)
        ]

    part = rows // NZ
    rest = part - FIRST
    paired = local.reshape(NX, NC, NZ, part, cols)
    others = lax.dynamic_index_in_dim(paired, 1 - core, 1, keepdims=False)
    kept = lax.dynamic_index_in_dim(paired, core, 1, keepdims=False)
    came = lax.ppermute(others.astype(jnp.float32), "dp", swap)
    chip = kept.astype(jnp.float32) + came

    def towards(shift):
        near = lax.dynamic_index_in_dim(chip, (x + shift) % NX, 0, keepdims=False)
        return near[:, :FIRST].reshape(NZ * FIRST, cols)

    cut = NZ * FIRST // 2
    far = towards(2)
    far_up = lax.ppermute(far[:cut], "dp", along(1))
    far_down = lax.ppermute(far[cut:], "dp", along(-1))
    late = jnp.transpose(chip[:, :, FIRST:], (1, 0, 2, 3)).reshape(NZ, NX * rest, cols)
    late = exchange(late, along_z)
    up, down = towards(1), towards(3)
    up = jnp.concatenate([up[:cut] + far_up, up[cut:]], axis=0)
    down = jnp.concatenate([down[:cut], down[cut:] + far_down], axis=0)
    from_up = lax.ppermute(up, "dp", along(1))
    from_down = lax.ppermute(down, "dp", along(-1))
    over_x = towards(0) + from_up + from_down
    over_z = jnp.sum(exchange(over_x.reshape(NZ, FIRST, cols), along_z), axis=0)
    mean = over_z * (1.0 / groups)
    late = jnp.sum(late, axis=0)
    late = (late + lax.ppermute(late, "dp", along(1))) + (
        lax.ppermute(late, "dp", along(-1)) + lax.ppermute(late, "dp", along(2))
    )
    late = (late * (1.0 / groups)).reshape(NX, rest, cols)
    other = lax.ppermute(late, "dp", swap)
    late = jnp.stack(
        [jnp.where(core == 0, late, other), jnp.where(core == 0, other, late)], axis=1
    ).reshape(count, rest, cols)
    everything = exchange(jnp.broadcast_to(mean[None], (count, FIRST, cols)), across)
    everything = jnp.concatenate([everything, late], axis=1)
    outgoing = jnp.take(everything, wanted, axis=0, mode="clip")
    return [exchange(outgoing.reshape(NZ, SLOTS, part, cols), along_z)]


def body(partials, owner, rowblock, factor, basis, moment1, moment2, master):
    groups = lax.axis_size("dp")
    cols = lax.axis_size("mp")
    d = lax.axis_index("dp")
    y = lax.axis_index("mp")
    core = d % NC
    count = owner.shape[0]
    rows = factor.shape[1]
    order = jnp.arange(count)
    same = owner[:, None] == owner[None, :]
    slot = jnp.sum((same & (order[None, :] < order[:, None])).astype(jnp.int32), axis=1)
    mine = (owner[None, :] == d) & (slot[None, :] == jnp.arange(SLOTS)[:, None])
    valid = jnp.any(mine, axis=1)
    my_matrix = jnp.sum(jnp.where(mine, order[None, :], 0), axis=1)

    everyone = [(g, j) for g in range(groups) for j in range(cols)]

    def ring(shift, parity):
        return [
            (g * cols + j, g * cols + (j + shift) % cols)
            for g, j in everyone
            if parity is None or (j - g) % 2 == parity
        ]

    def move(v, shift, parity=None):
        return lax.ppermute(v, ("dp", "mp"), ring(shift, parity))

    def target_slot(at):
        return ((at - core) % cols) // 2

    even = (y - core) % 2 == 0
    own_slot = target_slot(y)
    left_slot = target_slot(y - 1)

    def to_targets(pick):
        back = pick(jnp.where(even, 1 - own_slot, left_slot))
        return pick(own_slot), move(back, -1, 1), move(back, 2, 0), move(pick(1 - left_slot), 1, 1)

    keep = jnp.where(own_slot == 0, valid[0], valid[1])
    scalars = jnp.stack([y, own_slot, keep.astype(jnp.int32)]).astype(jnp.int32)
    basis_rows = jnp.concatenate([basis[0, :, 0], basis[0, :, 1]], axis=1)
    blocks = (basis_rows, move(basis_rows, -1), move(basis_rows, 2), move(basis_rows, 1))
    halves = prepare(scalars, blocks)
    factors = to_targets(lambda s: jnp.where(s == 0, factor[0, :, 0], factor[0, :, 1]))

    incoming = owned_gradients(partials[0], owner, slot, d)

    def block_of(s):
        return jnp.concatenate(
            [
                jnp.where(s == 0, v[:, 0], v[:, 1]).reshape(-1, v.shape[-1])
                for v in incoming
            ],
            axis=0,
        )

    pieces = to_targets(block_of)
    chosen = jnp.sum(jnp.where(mine[:, :, None], rowblock[None], 0), axis=1)
    sent = update(chosen, incoming, halves, moment1[0], moment2[0], master[0])
    received = lax.all_to_all(sent, "dp", split_axis=0, concat_axis=0, tiled=True)
    own, after, across, before = refresh(scalars, pieces, factors, halves[0], halves[1])

    block_rows = rows * cols // groups
    landed = jnp.take(received, owner, axis=0, mode="clip")
    train_weights = jnp.where(
        (slot == 0)[:, None, None], landed[:, :block_rows], landed[:, block_rows:2 * block_rows]
    )[:, None]

    from_left = move(after, 1, 0)
    from_far = move(across, 2, 0)
    from_right = move(before, -1, 0)
    near = jnp.where(even, own, from_left)
    far = jnp.where(even, from_far, from_right)
    near_first = jnp.where(even, own_slot, left_slot) == 0
    new_basis = jnp.stack(
        [jnp.where(near_first, near, far), jnp.where(near_first, far, near)], axis=1
    )
    return (train_weights, new_basis[None])


def solution(mesh):
    placed = (
        P("dp", None, None, "mp"),
        P(),
        P(),
        P("dp", "mp", None, None),
        P("dp", "mp", None, None),
        P("dp", None, None, "mp"),
        P("dp", None, None, "mp"),
        P("dp", None, None, "mp"),
    )

    return jax.shard_map(
        body,
        mesh=mesh,
        in_specs=placed,
        out_specs=(P(None, "dp", None, "mp"), P("dp", "mp", None, None)),
        check_vma=False,
    )
```

```python
import jax
import jax.numpy as jnp
from jax import lax
from jax.experimental import pallas as pl
from jax.experimental.pallas import tpu as pltpu
from jax.sharding import PartitionSpec as P


NS_ITERS = 4
SLOTS = 2
BLOCK = 256
FIRST = 72
VMEM = 63 << 20
PARTS = (80,)
NX, NZ, NC = 4, 8, 2
NT = (((1,), (1,)), ((), ()))
NN = (((1,), (0,)), ((), ()))


def split(x):
    hi = x.astype(jnp.bfloat16)
    lo = (x - hi.astype(jnp.float32)).astype(jnp.bfloat16)
    return hi, lo


def mm(left, right, dims):
    return lax.dot_general(left, right, dims, preferred_element_type=jnp.float32)


def mm3(left, right, dims=NN):
    (lh, ll), (rh, rl) = left, right
    return mm(lh, rh, dims) + (mm(lh, rl, dims) + mm(ll, rh, dims))


def row_starts(y, rows, cols):
    return [pl.multiple_of(lax.rem(y + k, cols) * rows, 32) for k in range(cols)]


def scattered(part):
    lead = sum(PARTS[:part])
    whole = sum(PARTS)
    return [(z * PARTS[part], z * whole + lead, PARTS[part]) for z in range(NZ)]


def start_all(copies):
    for copy in copies:
        copy.start()


def wait_all(copies):
    for copy in copies:
        copy.wait()


def prepare_kernel(at, b0, b1, b2, b3, hi_ref, lo_ref, thi_ref, tlo_ref, held, whole, parts, in_sem, out_sem):
    blocks = (b0, b1, b2, b3)
    rows, d = b0.shape[0], whole.shape[0]
    fetch = [pltpu.make_async_copy(b, held.at[k], in_sem.at[k]) for k, b in enumerate(blocks)]
    start_all(fetch)
    wait_all(fetch)
    starts = row_starts(at[0], rows, len(blocks))
    stores = []
    for s in range(SLOTS):
        for k, start in enumerate(starts):
            whole[pl.ds(start, rows), :] = held[k, :, s * d:(s + 1) * d]
        b = whole[...]
        parts[0, s], parts[1, s] = split(b)
        parts[2, s], parts[3, s] = split(b.T)
        mine = [
            pltpu.make_async_copy(parts.at[k, s], ref.at[s], out_sem.at[k, s])
            for k, ref in enumerate((hi_ref, lo_ref, thi_ref, tlo_ref))
        ]
        start_all(mine)
        stores += mine
    wait_all(stores)


def prepare(scalars, blocks):
    rows, wide = blocks[0].shape
    d = wide // SLOTS
    half = jax.ShapeDtypeStruct((SLOTS, d, d), jnp.bfloat16)
    hbm = pl.BlockSpec(memory_space=pltpu.HBM)
    return pl.pallas_call(
        prepare_kernel,
        out_shape=[half] * 4,
        in_specs=[pl.BlockSpec(memory_space=pltpu.SMEM)] + [hbm] * 4,
        out_specs=[hbm] * 4,
        scratch_shapes=[
            pltpu.VMEM((4, rows, wide), jnp.float32),
            pltpu.VMEM((d, d), jnp.float32),
            pltpu.VMEM((4, SLOTS, d, d), jnp.bfloat16),
            pltpu.SemaphoreType.DMA((4,)),
            pltpu.SemaphoreType.DMA((4, SLOTS)),
        ],
        compiler_params=pltpu.CompilerParams(vmem_limit_bytes=VMEM),
        cost_estimate=pl.CostEstimate(flops=8 * d * d, bytes_accessed=24 * d * d, transcendentals=0),
        name="prepare",
    )(scalars, *blocks)


def update_kernel(chosen, *refs):
    count = len(PARTS)
    incoming, sources, states, out = refs[:count], refs[count:count + 4], refs[count + 4:count + 7], refs[count + 7]
    scratch = refs[count + 8:]
    came, (parts, state, gh, gl, weights, came_sem, part_sem, state_sem) = scratch[:count], scratch[count:]
    groups = out.shape[0]
    block = state.shape[2] // groups
    order = (2, 3, 0, 1)
    get_came = [pltpu.make_async_copy(r, c, came_sem.at[k]) for k, (r, c) in enumerate(zip(incoming, came))]
    get_part = [
        [pltpu.make_async_copy(sources[k].at[s], parts.at[k, s], part_sem.at[k, s]) for k in order]
        for s in range(SLOTS)
    ]
    get_state = [
        [pltpu.make_async_copy(r.at[s], state.at[k, s], state_sem.at[k, s]) for k, r in enumerate(states)]
        for s in range(SLOTS)
    ]
    start_all(get_came)
    for s in range(SLOTS):
        start_all(get_part[s])
        start_all(get_state[s])
    wait_all(get_came)
    for s in range(SLOTS):
        for part, ref in enumerate(came):
            for z, (_, row, size) in enumerate(scattered(part)):
                gh[row:row + size], gl[row:row + size] = split(ref[z, s])
        wait_all(get_part[s][:2])
        turned = mm3((parts[2, s], parts[3, s]), (gh[...], gl[...]))
        wait_all(get_state[s])
        first = 0.9 * state[0, s] + 0.1 * turned
        second = 0.95 * state[1, s] + 0.05 * turned * turned
        wait_all(get_part[s][2:])
        direction = mm3((parts[0, s], parts[1, s]), split(first / (jnp.sqrt(second) + 1e-08)))
        fresh = state[2, s] - 0.1 * (direction + 0.1 * state[2, s])
        here = slice(s * block, (s + 1) * block)
        for j in range(groups):
            weights[j, here, :] = fresh[j * block:(j + 1) * block]

        def send(j, carry):
            out[j, here, :] = weights[chosen[s, j], here, :]
            return carry

        lax.fori_loop(0, groups, send, 0, unroll=4)


def update(chosen, incoming, halves, m1, m2, held):
    groups = chosen.shape[1]
    d, cols = m1.shape[1:]
    block = d // groups
    padded = -(-SLOTS * block // 8) * 8
    hbm = pl.BlockSpec(memory_space=pltpu.HBM)
    return pl.pallas_call(
        update_kernel,
        out_shape=jax.ShapeDtypeStruct((groups, padded, cols), jnp.float32),
        in_specs=[pl.BlockSpec(memory_space=pltpu.SMEM)] + [hbm] * (7 + len(PARTS)),
        out_specs=pl.BlockSpec(memory_space=pltpu.VMEM),
        scratch_shapes=[pltpu.VMEM(v.shape, jnp.float32) for v in incoming]
        + [
            pltpu.VMEM((4, SLOTS, d, d), jnp.bfloat16),
            pltpu.VMEM((3, SLOTS, d, cols), jnp.float32),
            pltpu.VMEM((d, cols), jnp.bfloat16),
            pltpu.VMEM((d, cols), jnp.bfloat16),
            pltpu.VMEM((groups, padded, cols), jnp.float32),
            pltpu.SemaphoreType.DMA((len(PARTS),)),
            pltpu.SemaphoreType.DMA((4, SLOTS)),
            pltpu.SemaphoreType.DMA((3, SLOTS)),
        ],
        compiler_params=pltpu.CompilerParams(vmem_limit_bytes=VMEM),
        cost_estimate=pl.CostEstimate(
            flops=24 * d * d * cols, bytes_accessed=36 * d * cols, transcendentals=2 * d * cols
        ),
        name="update",
    )(chosen, *incoming, *halves, m1, m2, held)


def refresh_kernel(
    at, came, g1, g2, g3, f0, f1, f2, f3, b_hi, b_lo, o0, o1, o2, o3,
    g_in, f_in, gbuf, xbuf, abuf, stack, x_ref, a_ref, own_sem, g_sem, f_sem, b_sem,
):
    d = x_ref.shape[0]
    w = g1.shape[1]
    kc = 4 * w
    rows = f0.shape[0]
    part = came.shape[2]
    get_own = [
        pltpu.make_async_copy(came.at[z, at[1]], g_in.at[0, pl.ds(z * part, part)], own_sem.at[z])
        for z in range(NZ)
    ]
    get_g = [get_own] + [
        [pltpu.make_async_copy(r, g_in.at[k + 1], g_sem.at[k])] for k, r in enumerate((g1, g2, g3))
    ]
    get_f = [
        pltpu.make_async_copy(r, f_in.at[pl.ds(start, rows)], f_sem.at[k])
        for k, (r, start) in enumerate(zip((f0, f1, f2, f3), row_starts(at[0], rows, 4)))
    ]
    get_b = [
        pltpu.make_async_copy(r.at[at[1]], stack.at[pl.ds(k * d, d)], b_sem.at[k])
        for k, r in enumerate((b_hi, b_hi, b_lo))
    ]
    for copies in get_g:
        start_all(copies)
    start_all(get_f)
    start_all(get_b)

    def put(buf, k, v, r=0, c=0):
        hi, lo = split(v)
        n, m = v.shape
        buf[r:r + n, c:c + m] = lo
        buf[r:r + n, k + c:k + c + m] = hi
        buf[r:r + n, 2 * k + c:2 * k + c + m] = hi
        return hi, lo

    def gram(buf, k, use):
        for c in range(0, d, BLOCK):
            e = min(c + BLOCK, d)
            p = mm(buf[c:, :2 * k], buf[c:e, k:], NT) + mm(buf[c:, k:2 * k], buf[c:e, :k], NT)
            use(p, c, c)
            if e < d:
                use(p[e - c:].T, c, e)

    def times_stack():
        return mm(abuf[:, :2 * d], stack[:2 * d], NN) + mm(abuf[:, d:2 * d], stack[2 * d:], NN)

    for b in range(4):
        wait_all(get_g[b])
        base = 0
        for part in range(len(PARTS)):
            for source, row, size in scattered(part):
                put(gbuf, kc, g_in[b, base + source:base + source + size], row, b * w)
            base += NZ * PARTS[part]
    wait_all(get_f)

    def use_outer(v, r, c):
        n, m = v.shape
        put(abuf, d, 0.95 * f_in[r:r + n, c:c + m] + 0.05 * v, r, c)

    gram(gbuf, kc, use_outer)
    wait_all(get_b)
    power = times_stack()
    total = jnp.sum(power * power)
    x_ref[...] = power / jnp.sqrt(jnp.full((1, 1), total + 1e-06, jnp.float32))

    def step(_, carry):
        hi, lo = put(xbuf, d, x_ref[...])
        stack[:d] = hi
        stack[d:2 * d] = hi
        stack[2 * d:] = lo

        def use_inner(v, r, c):
            n, m = v.shape
            a_ref[r:r + n, c:c + m] = v
            put(abuf, d, v, r, c)

        def use_squared(v, r, c):
            n, m = v.shape
            a_ref[r:r + n, c:c + m] = -4.775 * a_ref[r:r + n, c:c + m] + 2.0315 * v

        gram(xbuf, d, use_inner)
        gram(abuf, d, use_squared)
        hi, lo = split(a_ref[...])
        abuf[:, :d] = lo
        abuf[:, d:2 * d] = hi
        x_ref[...] = 3.4445 * x_ref[...] + times_stack()
        return carry

    lax.fori_loop(0, NS_ITERS, step, 0)
    for start, o_ref in zip(row_starts(at[0], rows, 4), (o0, o1, o2, o3)):
        o_ref[...] = jnp.where(at[2] > 0, x_ref[pl.ds(start, rows), :], 0.0)


def refresh(scalars, pieces, factors, b_hi, b_lo):
    d = factors[0].shape[1]
    w = pieces[1].shape[1]
    hbm = pl.BlockSpec(memory_space=pltpu.HBM)
    return pl.pallas_call(
        refresh_kernel,
        out_shape=[jax.ShapeDtypeStruct(factors[0].shape, jnp.float32)] * 4,
        in_specs=[pl.BlockSpec(memory_space=pltpu.SMEM)] + [hbm] * 10,
        out_specs=[pl.BlockSpec(memory_space=pltpu.VMEM)] * 4,
        scratch_shapes=[
            pltpu.VMEM((4, d, w), jnp.float32),
            pltpu.VMEM((d, d), jnp.float32),
            pltpu.VMEM((d, 12 * w), jnp.bfloat16),
            pltpu.VMEM((d, 3 * d), jnp.bfloat16),
            pltpu.VMEM((d, 3 * d), jnp.bfloat16),
            pltpu.VMEM((3 * d, d), jnp.bfloat16),
            pltpu.VMEM((d, d), jnp.float32),
            pltpu.VMEM((d, d), jnp.float32),
            pltpu.SemaphoreType.DMA((NZ,)),
            pltpu.SemaphoreType.DMA((3,)),
            pltpu.SemaphoreType.DMA((4,)),
            pltpu.SemaphoreType.DMA((3,)),
        ],
        compiler_params=pltpu.CompilerParams(vmem_limit_bytes=44 << 20),
        cost_estimate=pl.CostEstimate(
            flops=6 * 10 * d**3, bytes_accessed=16 * d * d, transcendentals=0
        ),
        name="refresh",
    )(scalars, *(pltpu.with_memory_space_constraint(v, pltpu.HBM) for v in (*pieces, *factors, b_hi, b_lo)))


def line(x, z, core):
    return (x * NZ + z) * NC + core


def owned_gradients(local, owner, slot, d):
    x, core = d // (NZ * NC), d % NC
    count, rows, cols = local.shape
    groups = NX * NZ * NC
    along_z = [[line(a, b, c) for b in range(NZ)] for a in range(NX) for c in range(NC)]
    across = [[line(a, b, c) for a in range(NX) for c in range(NC)] for b in range(NZ)]
    swap = [
        (line(a, b, c), line(a, b, 1 - c))
        for a in range(NX) for b in range(NZ) for c in range(NC)
    ]

    def exchange(v, lines):
        return lax.all_to_all(v, "dp", 0, 0, axis_index_groups=lines, tiled=True)

    hits = (owner[None, None, :] == jnp.arange(groups)[:, None, None]) & (
        slot[None, None, :] == jnp.arange(SLOTS)[None, :, None]
    )
    matrix_of = jnp.sum(jnp.where(hits, jnp.arange(count)[None, None, :], 0), axis=2)
    wanted = lax.dynamic_index_in_dim(matrix_of.reshape(NX, NZ, NC, SLOTS), x, 0, keepdims=False)
    wanted = lax.dynamic_index_in_dim(wanted, core, 1, keepdims=False).reshape(-1)

    def along(shift):
        return [
            (line(a, b, c), line((a + shift) % NX, b, c))
            for a in range(NX) for b in range(NZ) for c in range(NC)
        ]

    part = rows // NZ
    rest = part - FIRST
    paired = local.reshape(NX, NC, NZ, part, cols)
    others = lax.dynamic_index_in_dim(paired, 1 - core, 1, keepdims=False)
    kept = lax.dynamic_index_in_dim(paired, core, 1, keepdims=False)
    came = lax.ppermute(others.astype(jnp.float32), "dp", swap)
    chip = kept.astype(jnp.float32) + came

    def towards(shift):
        near = lax.dynamic_index_in_dim(chip, (x + shift) % NX, 0, keepdims=False)
        return near[:, :FIRST].reshape(NZ * FIRST, cols)

    cut = NZ * FIRST // 2
    far, up, down, home = towards(2), towards(1), towards(3), towards(0)
    far_up = lax.ppermute(far[:cut], "dp", along(1))
    far_down = lax.ppermute(far[cut:], "dp", along(-1))
    up_late = lax.ppermute(up[cut:], "dp", along(1))
    down_early = lax.ppermute(down[:cut], "dp", along(-1))
    late = jnp.transpose(chip[:, :, FIRST:], (1, 0, 2, 3)).reshape(NZ, NX * rest, cols)
    late = exchange(late, along_z)
    up_early = lax.ppermute(up[:cut] + far_up, "dp", along(1))
    down_late = lax.ppermute(down[cut:] + far_down, "dp", along(-1))
    over_x = jnp.concatenate(
        [home[:cut] + up_early + down_early, home[cut:] + up_late + down_late], axis=0
    )
    over_z = jnp.sum(exchange(over_x.reshape(NZ, FIRST, cols), along_z), axis=0)
    mean = over_z * (1.0 / groups)
    late = jnp.sum(late, axis=0)
    late = (late + lax.ppermute(late, "dp", along(1))) + (
        lax.ppermute(late, "dp", along(-1)) + lax.ppermute(late, "dp", along(2))
    )
    late = (late * (1.0 / groups)).reshape(NX, rest, cols)
    other = lax.ppermute(late, "dp", swap)
    late = jnp.stack(
        [jnp.where(core == 0, late, other), jnp.where(core == 0, other, late)], axis=1
    ).reshape(count, rest, cols)
    everything = exchange(jnp.broadcast_to(mean[None], (count, FIRST, cols)), across)
    everything = jnp.concatenate([everything, late], axis=1)
    outgoing = jnp.take(everything, wanted, axis=0, mode="clip")
    return [exchange(outgoing.reshape(NZ, SLOTS, part, cols), along_z)]


def body(partials, owner, rowblock, factor, basis, moment1, moment2, master):
    groups = lax.axis_size("dp")
    cols = lax.axis_size("mp")
    d = lax.axis_index("dp")
    y = lax.axis_index("mp")
    core = d % NC
    count = owner.shape[0]
    rows = factor.shape[1]
    order = jnp.arange(count)
    same = owner[:, None] == owner[None, :]
    slot = jnp.sum((same & (order[None, :] < order[:, None])).astype(jnp.int32), axis=1)
    mine = (owner[None, :] == d) & (slot[None, :] == jnp.arange(SLOTS)[:, None])
    valid = jnp.any(mine, axis=1)
    my_matrix = jnp.sum(jnp.where(mine, order[None, :], 0), axis=1)

    everyone = [(g, j) for g in range(groups) for j in range(cols)]

    def ring(shift, parity):
        return [
            (g * cols + j, g * cols + (j + shift) % cols)
            for g, j in everyone
            if parity is None or (j - g) % 2 == parity
        ]

    def move(v, shift, parity=None):
        return lax.ppermute(v, ("dp", "mp"), ring(shift, parity))

    def target_slot(at):
        return ((at - core) % cols) // 2

    even = (y - core) % 2 == 0
    own_slot = target_slot(y)
    left_slot = target_slot(y - 1)

    def to_targets(own, pick):
        back = pick(jnp.where(even, 1 - own_slot, left_slot))
        return own, move(back, -1, 1), move(back, 2, 0), move(pick(1 - left_slot), 1, 1)

    keep = jnp.where(own_slot == 0, valid[0], valid[1])
    scalars = jnp.stack([y, own_slot, keep.astype(jnp.int32)]).astype(jnp.int32)
    basis_rows = jnp.concatenate([basis[0, :, 0], basis[0, :, 1]], axis=1)
    blocks = (basis_rows, move(basis_rows, -1), move(basis_rows, 2), move(basis_rows, 1))
    halves = prepare(scalars, blocks)

    def factor_of(s):
        return jnp.where(s == 0, factor[0, :, 0], factor[0, :, 1])

    factors = to_targets(factor_of(own_slot), factor_of)

    incoming = owned_gradients(partials[0], owner, slot, d)

    def block_of(s):
        return jnp.concatenate(
            [
                jnp.where(s == 0, v[:, 0], v[:, 1]).reshape(-1, v.shape[-1])
                for v in incoming
            ],
            axis=0,
        )

    pieces = to_targets(incoming[0], block_of)
    chosen = jnp.sum(jnp.where(mine[:, :, None], rowblock[None], 0), axis=1)
    sent = update(chosen, incoming, halves, moment1[0], moment2[0], master[0])
    received = lax.all_to_all(sent, "dp", split_axis=0, concat_axis=0, tiled=True)
    own, after, across, before = refresh(scalars, pieces, factors, halves[0], halves[1])

    block_rows = rows * cols // groups
    landed = jnp.take(received, owner, axis=0, mode="clip")
    train_weights = jnp.where(
        (slot == 0)[:, None, None], landed[:, :block_rows], landed[:, block_rows:2 * block_rows]
    )[:, None]

    from_left = move(after, 1, 0)
    from_far = move(across, 2, 0)
    from_right = move(before, -1, 0)
    near = jnp.where(even, own, from_left)
    far = jnp.where(even, from_far, from_right)
    near_first = jnp.where(even, own_slot, left_slot) == 0
    new_basis = jnp.stack(
        [jnp.where(near_first, near, far), jnp.where(near_first, far, near)], axis=1
    )
    return (train_weights, new_basis[None])


def solution(mesh):
    placed = (
        P("dp", None, None, "mp"),
        P(),
        P(),
        P("dp", "mp", None, None),
        P("dp", "mp", None, None),
        P("dp", None, None, "mp"),
        P("dp", None, None, "mp"),
        P("dp", None, None, "mp"),
    )

    return jax.shard_map(
        body,
        mesh=mesh,
        in_specs=placed,
        out_specs=(P(None, "dp", None, "mp"), P("dp", "mp", None, None)),
        check_vma=False,
    )
```

```python
import jax
import jax.numpy as jnp
from jax import lax
from jax.experimental import pallas as pl
from jax.experimental.pallas import tpu as pltpu
from jax.sharding import PartitionSpec as P


NS_ITERS = 4
SLOTS = 2
BLOCK = 256
FIRST = 64
VMEM = 63 << 20
PARTS = (80,)
NX, NZ, NC = 4, 8, 2
NT = (((1,), (1,)), ((), ()))
NN = (((1,), (0,)), ((), ()))


def split(x):
    hi = x.astype(jnp.bfloat16)
    lo = (x - hi.astype(jnp.float32)).astype(jnp.bfloat16)
    return hi, lo


def mm(left, right, dims):
    return lax.dot_general(left, right, dims, preferred_element_type=jnp.float32)


def mm3(left, right, dims=NN):
    (lh, ll), (rh, rl) = left, right
    return mm(lh, rh, dims) + (mm(lh, rl, dims) + mm(ll, rh, dims))


def row_starts(y, rows, cols):
    return [pl.multiple_of(lax.rem(y + k, cols) * rows, 32) for k in range(cols)]


def scattered(part):
    lead = sum(PARTS[:part])
    whole = sum(PARTS)
    return [(z * PARTS[part], z * whole + lead, PARTS[part]) for z in range(NZ)]


def start_all(copies):
    for copy in copies:
        copy.start()


def wait_all(copies):
    for copy in copies:
        copy.wait()


def prepare_kernel(at, b0, b1, b2, b3, hi_ref, lo_ref, thi_ref, tlo_ref, held, whole, parts, in_sem, out_sem):
    blocks = (b0, b1, b2, b3)
    rows, d = b0.shape[0], whole.shape[0]
    fetch = [pltpu.make_async_copy(b, held.at[k], in_sem.at[k]) for k, b in enumerate(blocks)]
    start_all(fetch)
    wait_all(fetch)
    starts = row_starts(at[0], rows, len(blocks))
    stores = []
    for s in range(SLOTS):
        for k, start in enumerate(starts):
            whole[pl.ds(start, rows), :] = held[k, :, s * d:(s + 1) * d]
        b = whole[...]
        parts[0, s], parts[1, s] = split(b)
        parts[2, s], parts[3, s] = split(b.T)
        mine = [
            pltpu.make_async_copy(parts.at[k, s], ref.at[s], out_sem.at[k, s])
            for k, ref in enumerate((hi_ref, lo_ref, thi_ref, tlo_ref))
        ]
        start_all(mine)
        stores += mine
    wait_all(stores)


def prepare(scalars, blocks):
    rows, wide = blocks[0].shape
    d = wide // SLOTS
    half = jax.ShapeDtypeStruct((SLOTS, d, d), jnp.bfloat16)
    hbm = pl.BlockSpec(memory_space=pltpu.HBM)
    return pl.pallas_call(
        prepare_kernel,
        out_shape=[half] * 4,
        in_specs=[pl.BlockSpec(memory_space=pltpu.SMEM)] + [hbm] * 4,
        out_specs=[hbm] * 4,
        scratch_shapes=[
            pltpu.VMEM((4, rows, wide), jnp.float32),
            pltpu.VMEM((d, d), jnp.float32),
            pltpu.VMEM((4, SLOTS, d, d), jnp.bfloat16),
            pltpu.SemaphoreType.DMA((4,)),
            pltpu.SemaphoreType.DMA((4, SLOTS)),
        ],
        compiler_params=pltpu.CompilerParams(vmem_limit_bytes=VMEM),
        cost_estimate=pl.CostEstimate(flops=8 * d * d, bytes_accessed=24 * d * d, transcendentals=0),
        name="prepare",
    )(scalars, *blocks)


def update_kernel(chosen, *refs):
    count = len(PARTS)
    incoming, sources, states, out = refs[:count], refs[count:count + 4], refs[count + 4:count + 7], refs[count + 7]
    scratch = refs[count + 8:]
    came, (parts, state, gh, gl, weights, came_sem, part_sem, state_sem) = scratch[:count], scratch[count:]
    groups = out.shape[0]
    block = state.shape[2] // groups
    order = (2, 3, 0, 1)
    get_came = [pltpu.make_async_copy(r, c, came_sem.at[k]) for k, (r, c) in enumerate(zip(incoming, came))]
    get_part = [
        [pltpu.make_async_copy(sources[k].at[s], parts.at[k, s], part_sem.at[k, s]) for k in order]
        for s in range(SLOTS)
    ]
    get_state = [
        [pltpu.make_async_copy(r.at[s], state.at[k, s], state_sem.at[k, s]) for k, r in enumerate(states)]
        for s in range(SLOTS)
    ]
    start_all(get_came)
    for s in range(SLOTS):
        start_all(get_part[s])
        start_all(get_state[s])
    wait_all(get_came)
    for s in range(SLOTS):
        for part, ref in enumerate(came):
            for z, (_, row, size) in enumerate(scattered(part)):
                gh[row:row + size], gl[row:row + size] = split(ref[z, s])
        wait_all(get_part[s][:2])
        turned = mm3((parts[2, s], parts[3, s]), (gh[...], gl[...]))
        wait_all(get_state[s])
        first = 0.9 * state[0, s] + 0.1 * turned
        second = 0.95 * state[1, s] + 0.05 * turned * turned
        wait_all(get_part[s][2:])
        direction = mm3((parts[0, s], parts[1, s]), split(first / (jnp.sqrt(second) + 1e-08)))
        fresh = state[2, s] - 0.1 * (direction + 0.1 * state[2, s])
        here = slice(s * block, (s + 1) * block)
        for j in range(groups):
            weights[j, here, :] = fresh[j * block:(j + 1) * block]

        def send(j, carry):
            out[j, here, :] = weights[chosen[s, j], here, :]
            return carry

        lax.fori_loop(0, groups, send, 0, unroll=4)


def update(chosen, incoming, halves, m1, m2, held):
    groups = chosen.shape[1]
    d, cols = m1.shape[1:]
    block = d // groups
    padded = -(-SLOTS * block // 8) * 8
    hbm = pl.BlockSpec(memory_space=pltpu.HBM)
    return pl.pallas_call(
        update_kernel,
        out_shape=jax.ShapeDtypeStruct((groups, padded, cols), jnp.float32),
        in_specs=[pl.BlockSpec(memory_space=pltpu.SMEM)] + [hbm] * (7 + len(PARTS)),
        out_specs=pl.BlockSpec(memory_space=pltpu.VMEM),
        scratch_shapes=[pltpu.VMEM(v.shape, jnp.float32) for v in incoming]
        + [
            pltpu.VMEM((4, SLOTS, d, d), jnp.bfloat16),
            pltpu.VMEM((3, SLOTS, d, cols), jnp.float32),
            pltpu.VMEM((d, cols), jnp.bfloat16),
            pltpu.VMEM((d, cols), jnp.bfloat16),
            pltpu.VMEM((groups, padded, cols), jnp.float32),
            pltpu.SemaphoreType.DMA((len(PARTS),)),
            pltpu.SemaphoreType.DMA((4, SLOTS)),
            pltpu.SemaphoreType.DMA((3, SLOTS)),
        ],
        compiler_params=pltpu.CompilerParams(vmem_limit_bytes=VMEM),
        cost_estimate=pl.CostEstimate(
            flops=24 * d * d * cols, bytes_accessed=36 * d * cols, transcendentals=2 * d * cols
        ),
        name="update",
    )(chosen, *incoming, *halves, m1, m2, held)


def refresh_kernel(
    at, came, g1, g2, g3, f0, f1, f2, f3, b_hi, b_lo, o0, o1, o2, o3,
    g_in, f_in, gbuf, xbuf, abuf, stack, x_ref, a_ref, own_sem, g_sem, f_sem, b_sem,
):
    d = x_ref.shape[0]
    w = g1.shape[1]
    kc = 4 * w
    rows = f0.shape[0]
    part = came.shape[2]
    get_own = [
        pltpu.make_async_copy(came.at[z, at[1]], g_in.at[0, pl.ds(z * part, part)], own_sem.at[z])
        for z in range(NZ)
    ]
    get_g = [get_own] + [
        [pltpu.make_async_copy(r, g_in.at[k + 1], g_sem.at[k])] for k, r in enumerate((g1, g2, g3))
    ]
    get_f = [
        pltpu.make_async_copy(r, f_in.at[pl.ds(start, rows)], f_sem.at[k])
        for k, (r, start) in enumerate(zip((f0, f1, f2, f3), row_starts(at[0], rows, 4)))
    ]
    get_b = [
        pltpu.make_async_copy(r.at[at[1]], stack.at[pl.ds(k * d, d)], b_sem.at[k])
        for k, r in enumerate((b_hi, b_hi, b_lo))
    ]
    for copies in get_g:
        start_all(copies)
    start_all(get_f)
    start_all(get_b)

    def put(buf, k, v, r=0, c=0):
        hi, lo = split(v)
        n, m = v.shape
        buf[r:r + n, c:c + m] = lo
        buf[r:r + n, k + c:k + c + m] = hi
        buf[r:r + n, 2 * k + c:2 * k + c + m] = hi
        return hi, lo

    def gram(buf, k, use):
        for c in range(0, d, BLOCK):
            e = min(c + BLOCK, d)
            p = mm(buf[c:, :2 * k], buf[c:e, k:], NT) + mm(buf[c:, k:2 * k], buf[c:e, :k], NT)
            use(p, c, c)
            if e < d:
                use(p[e - c:].T, c, e)

    def times_stack():
        return mm(abuf[:, :2 * d], stack[:2 * d], NN) + mm(abuf[:, d:2 * d], stack[2 * d:], NN)

    for b in range(4):
        wait_all(get_g[b])
        base = 0
        for part in range(len(PARTS)):
            for source, row, size in scattered(part):
                put(gbuf, kc, g_in[b, base + source:base + source + size], row, b * w)
            base += NZ * PARTS[part]
    wait_all(get_f)

    def use_outer(v, r, c):
        n, m = v.shape
        put(abuf, d, 0.95 * f_in[r:r + n, c:c + m] + 0.05 * v, r, c)

    gram(gbuf, kc, use_outer)
    wait_all(get_b)
    power = times_stack()
    total = jnp.sum(power * power)
    x_ref[...] = power / jnp.sqrt(jnp.full((1, 1), total + 1e-06, jnp.float32))

    def step(_, carry):
        hi, lo = put(xbuf, d, x_ref[...])
        stack[:d] = hi
        stack[d:2 * d] = hi
        stack[2 * d:] = lo

        def use_inner(v, r, c):
            n, m = v.shape
            a_ref[r:r + n, c:c + m] = v
            put(abuf, d, v, r, c)

        def use_squared(v, r, c):
            n, m = v.shape
            a_ref[r:r + n, c:c + m] = -4.775 * a_ref[r:r + n, c:c + m] + 2.0315 * v

        gram(xbuf, d, use_inner)
        gram(abuf, d, use_squared)
        hi, lo = split(a_ref[...])
        abuf[:, :d] = lo
        abuf[:, d:2 * d] = hi
        x_ref[...] = 3.4445 * x_ref[...] + times_stack()
        return carry

    lax.fori_loop(0, NS_ITERS, step, 0)
    for start, o_ref in zip(row_starts(at[0], rows, 4), (o0, o1, o2, o3)):
        o_ref[...] = jnp.where(at[2] > 0, x_ref[pl.ds(start, rows), :], 0.0)


def refresh(scalars, pieces, factors, b_hi, b_lo):
    d = factors[0].shape[1]
    w = pieces[1].shape[1]
    hbm = pl.BlockSpec(memory_space=pltpu.HBM)
    return pl.pallas_call(
        refresh_kernel,
        out_shape=[jax.ShapeDtypeStruct(factors[0].shape, jnp.float32)] * 4,
        in_specs=[pl.BlockSpec(memory_space=pltpu.SMEM)] + [hbm] * 10,
        out_specs=[pl.BlockSpec(memory_space=pltpu.VMEM)] * 4,
        scratch_shapes=[
            pltpu.VMEM((4, d, w), jnp.float32),
            pltpu.VMEM((d, d), jnp.float32),
            pltpu.VMEM((d, 12 * w), jnp.bfloat16),
            pltpu.VMEM((d, 3 * d), jnp.bfloat16),
            pltpu.VMEM((d, 3 * d), jnp.bfloat16),
            pltpu.VMEM((3 * d, d), jnp.bfloat16),
            pltpu.VMEM((d, d), jnp.float32),
            pltpu.VMEM((d, d), jnp.float32),
            pltpu.SemaphoreType.DMA((NZ,)),
            pltpu.SemaphoreType.DMA((3,)),
            pltpu.SemaphoreType.DMA((4,)),
            pltpu.SemaphoreType.DMA((3,)),
        ],
        compiler_params=pltpu.CompilerParams(vmem_limit_bytes=44 << 20),
        cost_estimate=pl.CostEstimate(
            flops=6 * 10 * d**3, bytes_accessed=16 * d * d, transcendentals=0
        ),
        name="refresh",
    )(scalars, *(pltpu.with_memory_space_constraint(v, pltpu.HBM) for v in (*pieces, *factors, b_hi, b_lo)))


def line(x, z, core):
    return (x * NZ + z) * NC + core


def owned_gradients(local, owner, slot, d):
    x, core = d // (NZ * NC), d % NC
    count, rows, cols = local.shape
    groups = NX * NZ * NC
    along_z = [[line(a, b, c) for b in range(NZ)] for a in range(NX) for c in range(NC)]
    across = [[line(a, b, c) for a in range(NX) for c in range(NC)] for b in range(NZ)]
    swap = [
        (line(a, b, c), line(a, b, 1 - c))
        for a in range(NX) for b in range(NZ) for c in range(NC)
    ]

    def exchange(v, lines):
        return lax.all_to_all(v, "dp", 0, 0, axis_index_groups=lines, tiled=True)

    hits = (owner[None, None, :] == jnp.arange(groups)[:, None, None]) & (
        slot[None, None, :] == jnp.arange(SLOTS)[None, :, None]
    )
    matrix_of = jnp.sum(jnp.where(hits, jnp.arange(count)[None, None, :], 0), axis=2)
    wanted = lax.dynamic_index_in_dim(matrix_of.reshape(NX, NZ, NC, SLOTS), x, 0, keepdims=False)
    wanted = lax.dynamic_index_in_dim(wanted, core, 1, keepdims=False).reshape(-1)

    def along(shift):
        return [
            (line(a, b, c), line((a + shift) % NX, b, c))
            for a in range(NX) for b in range(NZ) for c in range(NC)
        ]

    part = rows // NZ
    rest = part - FIRST
    paired = local.reshape(NX, NC, NZ, part, cols)
    others = lax.dynamic_index_in_dim(paired, 1 - core, 1, keepdims=False)
    kept = lax.dynamic_index_in_dim(paired, core, 1, keepdims=False)
    came = lax.ppermute(others.astype(jnp.float32), "dp", swap)
    chip = kept.astype(jnp.float32) + came

    def towards(shift):
        near = lax.dynamic_index_in_dim(chip, (x + shift) % NX, 0, keepdims=False)
        return near[:, :FIRST].reshape(NZ * FIRST, cols)

    cut = NZ * FIRST // 2
    far = towards(2)
    far_up = lax.ppermute(far[:cut], "dp", along(1))
    far_down = lax.ppermute(far[cut:], "dp", along(-1))
    late = jnp.transpose(chip[:, :, FIRST:], (1, 0, 2, 3)).reshape(NZ, NX * rest, cols)
    late = exchange(late, along_z)
    up, down = towards(1), towards(3)
    up = jnp.concatenate([up[:cut] + far_up, up[cut:]], axis=0)
    down = jnp.concatenate([down[:cut], down[cut:] + far_down], axis=0)
    from_up = lax.ppermute(up, "dp", along(1))
    from_down = lax.ppermute(down, "dp", along(-1))
    over_x = towards(0) + from_up + from_down
    over_z = jnp.sum(exchange(over_x.reshape(NZ, FIRST, cols), along_z), axis=0)
    mean = over_z * (1.0 / groups)
    late = jnp.sum(late, axis=0)
    late = (late + lax.ppermute(late, "dp", along(1))) + (
        lax.ppermute(late, "dp", along(-1)) + lax.ppermute(late, "dp", along(2))
    )
    late = (late * (1.0 / groups)).reshape(NX, rest, cols)
    other = lax.ppermute(late, "dp", swap)
    late = jnp.stack(
        [jnp.where(core == 0, late, other), jnp.where(core == 0, other, late)], axis=1
    ).reshape(count, rest, cols)
    everything = exchange(jnp.broadcast_to(mean[None], (count, FIRST, cols)), across)
    everything = jnp.concatenate([everything, late], axis=1)
    outgoing = jnp.take(everything, wanted, axis=0, mode="clip")
    return [exchange(outgoing.reshape(NZ, SLOTS, part, cols), along_z)]


def body(partials, owner, rowblock, factor, basis, moment1, moment2, master):
    groups = lax.axis_size("dp")
    cols = lax.axis_size("mp")
    d = lax.axis_index("dp")
    y = lax.axis_index("mp")
    core = d % NC
    count = owner.shape[0]
    rows = factor.shape[1]
    order = jnp.arange(count)
    same = owner[:, None] == owner[None, :]
    slot = jnp.sum((same & (order[None, :] < order[:, None])).astype(jnp.int32), axis=1)
    mine = (owner[None, :] == d) & (slot[None, :] == jnp.arange(SLOTS)[:, None])
    valid = jnp.any(mine, axis=1)
    my_matrix = jnp.sum(jnp.where(mine, order[None, :], 0), axis=1)

    everyone = [(g, j) for g in range(groups) for j in range(cols)]

    def ring(shift, parity):
        return [
            (g * cols + j, g * cols + (j + shift) % cols)
            for g, j in everyone
            if parity is None or (j - g) % 2 == parity
        ]

    def move(v, shift, parity=None):
        return lax.ppermute(v, ("dp", "mp"), ring(shift, parity))

    def target_slot(at):
        return ((at - core) % cols) // 2

    even = (y - core) % 2 == 0
    own_slot = target_slot(y)
    left_slot = target_slot(y - 1)

    def to_targets(own, pick):
        back = pick(jnp.where(even, 1 - own_slot, left_slot))
        return own, move(back, -1, 1), move(back, 2, 0), move(pick(1 - left_slot), 1, 1)

    keep = jnp.where(own_slot == 0, valid[0], valid[1])
    scalars = jnp.stack([y, own_slot, keep.astype(jnp.int32)]).astype(jnp.int32)
    basis_rows = jnp.concatenate([basis[0, :, 0], basis[0, :, 1]], axis=1)
    blocks = (basis_rows, move(basis_rows, -1), move(basis_rows, 2), move(basis_rows, 1))
    halves = prepare(scalars, blocks)

    def factor_of(s):
        return jnp.where(s == 0, factor[0, :, 0], factor[0, :, 1])

    factors = to_targets(factor_of(own_slot), factor_of)

    incoming = owned_gradients(partials[0], owner, slot, d)

    def block_of(s):
        return jnp.concatenate(
            [
                jnp.where(s == 0, v[:, 0], v[:, 1]).reshape(-1, v.shape[-1])
                for v in incoming
            ],
            axis=0,
        )

    pieces = to_targets(incoming[0], block_of)
    chosen = jnp.sum(jnp.where(mine[:, :, None], rowblock[None], 0), axis=1)
    sent = update(chosen, incoming, halves, moment1[0], moment2[0], master[0])
    received = lax.all_to_all(sent, "dp", split_axis=0, concat_axis=0, tiled=True)
    own, after, across, before = refresh(scalars, pieces, factors, halves[0], halves[1])

    block_rows = rows * cols // groups
    landed = jnp.take(received, owner, axis=0, mode="clip")
    train_weights = jnp.where(
        (slot == 0)[:, None, None], landed[:, :block_rows], landed[:, block_rows:2 * block_rows]
    )[:, None]

    from_left = move(after, 1, 0)
    from_far = move(across, 2, 0)
    from_right = move(before, -1, 0)
    near = jnp.where(even, own, from_left)
    far = jnp.where(even, from_far, from_right)
    near_first = jnp.where(even, own_slot, left_slot) == 0
    new_basis = jnp.stack(
        [jnp.where(near_first, near, far), jnp.where(near_first, far, near)], axis=1
    )
    return (train_weights, new_basis[None])


def solution(mesh):
    placed = (
        P("dp", None, None, "mp"),
        P(),
        P(),
        P("dp", "mp", None, None),
        P("dp", "mp", None, None),
        P("dp", None, None, "mp"),
        P("dp", None, None, "mp"),
        P("dp", None, None, "mp"),
    )

    return jax.shard_map(
        body,
        mesh=mesh,
        in_specs=placed,
        out_specs=(P(None, "dp", None, "mp"), P("dp", "mp", None, None)),
        check_vma=False,
    )
```
